1024 devices in a mesh: gx: 16 (over z), gy: 64 (over y, x, core).
Axes of the slice: x: 4, y: 8, z: 16, core: 2. Of those that a mesh axis runs over, the one named last changes fastest.
Arguments:
- pdf: float32 [19, 256, 8192], P(None, 'gx', 'gy'), as said below
- grains: float32 [26, 16, 16384], P(None, 'gx', 'gy'), as said below
- grain_moves: int32 [16, 16384], P('gx', 'gy'), may hold values from 0 to 8, as said below
- owner_map: int32 [32, 128], P('gx', 'gy'), may hold values from 0 to 15, as said below
- link_lists: int32 [3, 32, 32768], P(None, 'gx', 'gy'), may hold values from 0 to 511, as said below
Outputs:
- moved_blocks: float32 [256, 64, 19, 512], P('gx', 'gy')
- new_grains: float32 [26, 16, 20480], P(None, 'gx', 'gy')
The draws below stay inside these ranges and needn't reach their ends.
Inputs may be any that keep to these rules, and one draw needn't show every extreme that they name: `pdf`: each entry lies between 0.4 and 1.6 times its direction's lattice weight. `grains`: A grain's position lies inside the cells of the group that it belongs to after the move. `grain_moves`: at most 8 grains of one group move to any one of its eight neighbouring groups; every group moves at least one grain each way, and some group receives exactly 8 grains from each of its eight neighbours. `owner_map`: owners are gx indices in the block's own row of gy. At most 1 block of one group go to one owner, and in every row of gy one owner receives exactly 1 block from every group of that row. `link_lists`: row 0: a cell number of the block; row 1: a direction 1 to 18; row 2: a grain slot below 320. No cell appears twice among one block's links.
All inputs are finite; a program needn't handle non-finite values.
Results may differ from the reference program's by a relative error of at most 0.0003.
Values sent between devices are 32-bit elements; how exact they have to be, the bound alone decides.
No kernel may reach another device: no remote copies, remote signals or barrier semaphores. Data moves between devices by JAX's collectives and lax.ppermute only.
A program may use at most 64 MiB of HBM per device.

```python
import jax
import jax.numpy as jnp
import numpy as np
from jax import lax

Q = 19
GV = 26
E = 8
Z = 8
BXD = 2
BYD = 2
GR = 256
GCAP = 8
CAPP = 1
LB = 256
GROUP = 16
LANES = 64
BLK = 4
SLOTS = 16
CB = 512
GSLOT = 320
NBX = 32
NBY = 128
NX = 256
NY = 1024


lattice_wts = np.array([1.0 / 3.0] + [1.0 / 18.0] * 6 + [1.0 / 36.0] * 12, dtype=np.float32)


lattice_stepx = np.array([0, 1, -1, 0, 0, 0, 0, 1, -1, 1, -1, 1, -1, 1, -1, 0, 0, 0, 0], dtype=np.float32)


def draw_pdf(key, part):
    grid_shape = (Q, NX, NY * Z)
    weights = jnp.asarray(lattice_wts)[:, None, None]
    drift_term = jnp.asarray(lattice_stepx)[:, None, None]
    jitter = jax.random.uniform(key, grid_shape, jnp.float32, -1.0, 1.0)
    return weights * (1.0 + 0.15 * drift_term + 0.45 * jitter)


def draw_codes(key):
    base_key = jax.random.fold_in(key, 11)
    count_key, target_key, spread_key = jax.random.split(base_key, 3)
    counts = jax.random.randint(count_key, (GROUP, LANES, 9), GCAP // 2, GCAP + 1, jnp.int32)
    counts = counts.at[:, :, 4].set(0)
    aim_x = jax.random.randint(jax.random.fold_in(target_key, 1), (), 0, GROUP, jnp.int32)
    aim_y = jax.random.randint(jax.random.fold_in(target_key, 2), (), 0, LANES, jnp.int32)
    for move_code in (0, 1, 2, 3, 5, 6, 7, 8):
        counts = counts.at[(aim_x - (move_code // 3 - 1)) % GROUP, (aim_y - (move_code % 3 - 1)) % LANES, move_code].set(GCAP)
    group_keys = jax.random.split(spread_key, GROUP * LANES)
    flat_counts = counts.reshape(GROUP * LANES, 9)

    def one_group(group_key, group_counts):
        bounds = jnp.cumsum(group_counts, dtype=jnp.int32)
        ordinal = jnp.arange(GR, dtype=jnp.int32)
        sorted_codes = jnp.sum((ordinal[:, None] >= bounds[None, :]).astype(jnp.int32), axis=1, dtype=jnp.int32)
        sorted_codes = jnp.where(sorted_codes > 8, 4, sorted_codes)
        return jax.random.permutation(group_key, sorted_codes)
    grouped = jax.vmap(one_group)(group_keys, flat_counts)
    return grouped.reshape(GROUP, LANES, GR)


def draw_grain_moves(key, part):
    return draw_codes(key).reshape(GROUP, LANES * GR)


def draw_grains(key, part):
    grouped = draw_codes(key)
    dest_x = (jnp.arange(GROUP, dtype=jnp.int32)[:, None, None] + grouped // 3 - 1) % GROUP
    dest_y = (jnp.arange(LANES, dtype=jnp.int32)[None, :, None] + grouped % 3 - 1) % LANES
    float_key = jax.random.fold_in(key, 29)
    place_key, motion_key, remain_key = jax.random.split(float_key, 3)
    grid_shape = (GROUP, LANES, GR)
    fractions = jax.random.uniform(place_key, (3,) + grid_shape, jnp.float32)
    centre_x = (dest_x * (BXD * E)).astype(jnp.float32) + fractions[0] * (BXD * E)
    centre_y = (dest_y * (BYD * E)).astype(jnp.float32) + fractions[1] * (BYD * E)
    centre_z = fractions[2] * Z
    motion = jax.random.normal(motion_key, (6,) + grid_shape, jnp.float32)
    remaining = jax.random.normal(remain_key, (GV - 9,) + grid_shape, jnp.float32)
    scales = jnp.array([0.02, 0.02, 0.02, 0.0015, 0.0015, 0.0015], jnp.float32)[:, None, None, None]
    records = jnp.concatenate([jnp.stack([centre_x, centre_y, centre_z]), motion * scales, remaining], axis=0)
    return records.reshape(GV, GROUP, LANES * GR)


def draw_owner_map(key, part):
    heavy_owner = jax.random.randint(jax.random.fold_in(key, 5), (LANES,), 0, GROUP, jnp.int32)
    device_keys = jax.random.split(jax.random.fold_in(key, 6), GROUP * LANES)
    heavies = jnp.broadcast_to(heavy_owner[None, :], (GROUP, LANES)).reshape(-1)

    def one_device(device_key, chosen):
        first_key, second_key = jax.random.split(device_key)
        candidates = (chosen + 1 + jnp.arange(CAPP * (GROUP - 1), dtype=jnp.int32) // CAPP) % GROUP
        chosen_owners = jax.random.permutation(first_key, candidates)[:BLK - CAPP]
        heavy_part = jnp.full((CAPP,), chosen, jnp.int32)
        return jax.random.permutation(second_key, jnp.concatenate([heavy_part, chosen_owners]))
    owners = jax.vmap(one_device)(device_keys, heavies)
    return owners.reshape(GROUP, LANES, BXD, BYD).transpose(0, 2, 1, 3).reshape(GROUP * BXD, LANES * BYD)


def draw_link_lists(key, part):
    block_keys = jax.random.split(jax.random.fold_in(key, 7), NBX * NBY)

    def one_block(block_key):
        cell_key, dir_key, slot_key = jax.random.split(block_key, 3)
        cell_ids = jax.random.permutation(cell_key, CB)[:LB].astype(jnp.int32)
        direction_ids = jax.random.randint(dir_key, (LB,), 1, Q, jnp.int32)
        slot_ids = jax.random.randint(slot_key, (LB,), 0, GSLOT, jnp.int32)
        return jnp.stack([cell_ids, direction_ids, slot_ids])
    link_rows = jax.vmap(one_block)(block_keys)
    return link_rows.reshape(NBX, NBY, 3, LB).transpose(2, 0, 1, 3).reshape(3, NBX, NBY * LB)


def setup_inputs(seed: int = 0) -> dict:
    key_list = jax.random.split(jax.random.key(seed), 6)
    return {
        "pdf": draw_pdf(jax.random.fold_in(key_list[5], 71), 0),
        "grains": draw_grains(jax.random.fold_in(key_list[5], 71), 0),
        "grain_moves": draw_grain_moves(jax.random.fold_in(key_list[5], 71), 0),
        "owner_map": draw_owner_map(jax.random.fold_in(key_list[5], 71), 0),
        "link_lists": draw_link_lists(jax.random.fold_in(key_list[5], 71), 0),
    }


lattice_vel = np.array([[0, 0, 0], [1, 0, 0], [-1, 0, 0], [0, 1, 0], [0, -1, 0], [0, 0, 1], [0, 0, -1], [1, 1, 0], [-1, -1, 0], [1, -1, 0], [-1, 1, 0], [1, 0, 1], [-1, 0, -1], [1, 0, -1], [-1, 0, 1], [0, 1, 1], [0, -1, -1], [0, 1, -1], [0, -1, 1]], dtype=np.int32)
lattice_wts = np.array([1.0 / 3.0] + [1.0 / 18.0] * 6 + [1.0 / 36.0] * 12, dtype=np.float32)
opposite_dir = np.array([0, 2, 1, 4, 3, 6, 5, 8, 7, 10, 9, 12, 11, 14, 13, 16, 15, 18, 17], dtype=np.int32)
velocity_cols = lattice_vel.astype(np.float32)
moment_rows = np.stack([np.ones(19, np.float32), velocity_cols[:, 0], velocity_cols[:, 1], velocity_cols[:, 2], velocity_cols[:, 0] * velocity_cols[:, 0], velocity_cols[:, 1] * velocity_cols[:, 1], velocity_cols[:, 2] * velocity_cols[:, 2], velocity_cols[:, 0] * velocity_cols[:, 1], velocity_cols[:, 0] * velocity_cols[:, 2], velocity_cols[:, 1] * velocity_cols[:, 2]]).astype(np.float32)
viscosity_zero = 0.1
viscosity_limit = 0.01
relax_zero = 0.8
carreau_time = 20.0
carreau_power = 0.5

def collide(populations):
    moments = jnp.dot(jnp.asarray(moment_rows), populations, precision=lax.Precision.HIGHEST)
    density = moments[0]
    velocity = moments[1:4] / density
    projected = jnp.dot(jnp.asarray(velocity_cols), velocity, precision=lax.Precision.HIGHEST)
    speed_sq = lax.optimization_barrier(jnp.sum(velocity * velocity, axis=0))
    equilibrium = jnp.asarray(lattice_wts)[:, None] * density * (1.0 + 3.0 * projected + 4.5 * projected * projected - 1.5 * speed_sq)
    density_third = density / 3.0
    stress_xx = moments[4] - density_third - density * velocity[0] * velocity[0]
    stress_yy = moments[5] - density_third - density * velocity[1] * velocity[1]
    stress_zz = moments[6] - density_third - density * velocity[2] * velocity[2]
    stress_xy = moments[7] - density * velocity[0] * velocity[1]
    stress_xz = moments[8] - density * velocity[0] * velocity[2]
    stress_yz = moments[9] - density * velocity[1] * velocity[2]
    contracted = stress_xx * stress_xx + stress_yy * stress_yy + stress_zz * stress_zz + 2.0 * (stress_xy * stress_xy + stress_xz * stress_xz + stress_yz * stress_yz)
    shear_rate = 1.5 / (density * relax_zero) * jnp.sqrt(2.0 * contracted)
    viscosity = viscosity_limit + (viscosity_zero - viscosity_limit) * (1.0 + (carreau_time * shear_rate) ** 2) ** (0.5 * (carreau_power - 1.0))
    relax_time = 3.0 * viscosity + 0.5
    return populations - (populations - equilibrium) / relax_time

def pack_grains(own_grains, move_code, slot_cap):
    moving = move_code != 4
    region = jnp.where(move_code > 4, move_code - 1, move_code)
    matches = (move_code[None, :] == jnp.arange(9, dtype=jnp.int32)[:, None]).astype(jnp.int32)
    rank_of = lax.optimization_barrier(jnp.sum(matches * (jnp.cumsum(matches, axis=1, dtype=jnp.int32) - 1), axis=0, dtype=jnp.int32))
    target = region * slot_cap + rank_of
    placing = jnp.logical_and(target[:, None] == jnp.arange(8 * slot_cap, dtype=jnp.int32)[None, :], moving[:, None]).astype(jnp.float32)
    packed = jnp.dot(own_grains, placing, precision=lax.Precision.HIGHEST)
    kept_grains = own_grains * (move_code == 4).astype(jnp.float32)[None, :]
    return (kept_grains, packed)

def link_correction(cell_ids, direction_ids, picked, block_x, block_y):
    vel_table = jnp.asarray(velocity_cols)
    step_x = vel_table[:, 0][direction_ids]
    step_y = vel_table[:, 1][direction_ids]
    step_z = vel_table[:, 2][direction_ids]
    local_x = cell_ids // (E * Z)
    local_y = cell_ids // Z % E
    local_z = cell_ids % Z
    middle_x = (block_x * E + local_x).astype(jnp.float32) + 0.5 * step_x
    middle_y = (block_y * E + local_y).astype(jnp.float32) + 0.5 * step_y
    middle_z = local_z.astype(jnp.float32) + 0.5 * step_z
    rel_x = middle_x - picked[0]
    rel_y = middle_y - picked[1]
    rel_z = middle_z - picked[2]
    wall_x = picked[3] + picked[7] * rel_z - picked[8] * rel_y
    wall_y = picked[4] + picked[8] * rel_x - picked[6] * rel_z
    wall_z = picked[5] + picked[6] * rel_y - picked[7] * rel_x
    return 6.0 * jnp.asarray(lattice_wts)[direction_ids] * (step_x * wall_x + step_y * wall_y + step_z * wall_z)

def block_ranks(owners):
    count_blocks = owners.shape[-1]
    matching = owners[..., :, None] == owners[..., None, :]
    earlier = jnp.arange(count_blocks)[None, :] < jnp.arange(count_blocks)[:, None]
    return lax.optimization_barrier(jnp.sum(jnp.logical_and(matching, earlier).astype(jnp.int32), axis=-1, dtype=jnp.int32))

def set_values(row_values, target, values):
    return row_values.at[target].set(values)

def blockify(cells_grid):
    return cells_grid.reshape(Q, NBX, E, NBY, E, Z).transpose(1, 3, 0, 2, 4, 5).reshape(NBX, NBY, Q * CB)

def group_pack(own_grains, move_code):
    return pack_grains(own_grains, move_code, GCAP)

def reference(pdf, grains, grain_moves, owner_map, link_lists):
    grains_grid = grains.reshape(GV, GROUP, LANES, GR).transpose(1, 2, 0, 3)
    moves_grid = grain_moves.reshape(GROUP, LANES, GR)
    kept_grains, packed = jax.vmap(jax.vmap(group_pack))(grains_grid, moves_grid)
    regions = []
    for move_code in (0, 1, 2, 3, 5, 6, 7, 8):
        step_x = move_code // 3 - 1
        step_y = move_code % 3 - 1
        region = move_code if move_code < 4 else move_code - 1
        region_part = packed[:, :, :, region * GCAP:(region + 1) * GCAP]
        regions.append(jnp.roll(region_part, (step_x, step_y), axis=(0, 1)))
    grain_table = jnp.concatenate([kept_grains] + regions, axis=3).transpose(2, 0, 1, 3)
    new_grains = grain_table.reshape(GV, GROUP, LANES * GSLOT)
    slab_stack = jnp.moveaxis(pdf.reshape(Q, NBX, E * NY * Z), 1, 0)
    collided = jnp.moveaxis(lax.map(collide, slab_stack), 0, 1).reshape(Q, NX, NY, Z)
    passed = jnp.stack([jnp.roll(collided[direction], (int(lattice_vel[direction, 0]), int(lattice_vel[direction, 1]), int(lattice_vel[direction, 2])), axis=(0, 1, 2)) for direction in range(Q)])
    link_rows = link_lists.reshape(3, NBX, NBY, LB)
    cell_ids, direction_ids, grain_ids = (link_rows[0], link_rows[1], link_rows[2])
    column_x = jnp.arange(NBX, dtype=jnp.int32)[:, None, None]
    column_y = jnp.arange(NBY, dtype=jnp.int32)[None, :, None]
    picked = grain_table[:, column_x // BXD, column_y // BYD, grain_ids]
    correction = link_correction(cell_ids, direction_ids, picked, column_x, column_y)
    source = direction_ids * CB + cell_ids
    target = jnp.asarray(opposite_dir)[direction_ids] * CB + cell_ids
    star_blocks = blockify(collided)
    flow_blocks = blockify(passed)
    values = jnp.take_along_axis(star_blocks, source, axis=2) - correction
    final_blocks = jax.vmap(jax.vmap(set_values))(flow_blocks, target, values)
    owners = owner_map.reshape(GROUP, BXD, LANES, BYD).transpose(0, 2, 1, 3).reshape(GROUP, LANES, BLK)
    rank_of = block_ranks(owners)
    dest_row = owners * SLOTS + jnp.arange(GROUP, dtype=jnp.int32)[:, None, None] * CAPP + rank_of
    flat_dest = dest_row * LANES + jnp.arange(LANES, dtype=jnp.int32)[None, :, None]
    blocks_dev = final_blocks.reshape(GROUP, BXD, LANES, BYD, Q * CB).transpose(0, 2, 1, 3, 4).reshape(GROUP * LANES * BLK, Q * CB)
    total_blocks = GROUP * LANES * BLK
    source_of = jnp.full((GROUP * SLOTS * LANES,), total_blocks, jnp.int32).at[flat_dest.reshape(-1)].set(jnp.arange(total_blocks, dtype=jnp.int32))
    padded = jnp.concatenate([blocks_dev, jnp.zeros((1, Q * CB), blocks_dev.dtype)], axis=0)
    moved_blocks = padded[source_of].reshape(GROUP * SLOTS, LANES, Q, CB)
    return (moved_blocks, new_grains)
```

```python
import jax
import jax.numpy as jnp
import numpy as np
from jax import lax
from jax.experimental import pallas as pl
from jax.experimental.pallas import tpu as pltpu
from jax.sharding import PartitionSpec as P

Q = 19
E = 8
Z = 8
ROWS = 16
LANE = 128
GV = 26

CX = (0, 1, -1, 0, 0, 0, 0, 1, -1, 1, -1, 1, -1, 1, -1, 0, 0, 0, 0)
CY = (0, 0, 0, 1, -1, 0, 0, 1, -1, -1, 1, 0, 0, 0, 0, 1, -1, 1, -1)
CZ = (0, 0, 0, 0, 0, 1, -1, 0, 0, 0, 0, 1, -1, -1, 1, 1, -1, -1, 1)
OPP = (0, 2, 1, 4, 3, 6, 5, 8, 7, 10, 9, 12, 11, 14, 13, 16, 15, 18, 17)
WTS = tuple(float(np.float32(w)) for w in [1.0 / 3.0] + [1.0 / 18.0] * 6 + [1.0 / 36.0] * 12)
W6_AXIS = float(np.float32(6.0) * np.float32(1.0 / 18.0))
W6_DIAG = float(np.float32(6.0) * np.float32(1.0 / 36.0))
XUP = tuple(q for q in range(Q) if CX[q] == 1)
XDN = tuple(q for q in range(Q) if CX[q] == -1)
YUP = tuple(q for q in range(Q) if CY[q] == 1)
YDN = tuple(q for q in range(Q) if CY[q] == -1)
CODES = (0, 1, 2, 3, 5, 6, 7, 8)

F32 = jnp.float32
BF16 = jnp.bfloat16
I32 = jnp.int32


def iota(shape, dim):
    return lax.broadcasted_iota(I32, shape, dim)


def split3(value):
    high = value.astype(BF16)
    rest = value - high.astype(F32)
    middle = rest.astype(BF16)
    low = (rest - middle.astype(F32)).astype(BF16)
    return high, middle, low


def dot_nt(a, b):
    return lax.dot_general(a, b, (((1,), (1,)), ((), ())), preferred_element_type=F32)


def dot_nn(a, b):
    return lax.dot_general(a, b, (((1,), (0,)), ((), ())), preferred_element_type=F32)


def one_of(index, chosen):
    hit = index == chosen[0]
    for value in chosen[1:]:
        hit = jnp.logical_or(hit, index == value)
    return hit


def z_shift(plane, step, lane):
    depth = lane % Z
    if step == 1:
        return jnp.where(depth == 0, pltpu.roll(plane, LANE - (Z - 1), 1), pltpu.roll(plane, 1, 1))
    if step == -1:
        return jnp.where(depth == Z - 1, pltpu.roll(plane, Z - 1, 1), pltpu.roll(plane, LANE - 1, 1))
    return plane


def collide(f):
    s = {q: f[q] + f[q + 1] for q in range(1, Q, 2)}
    d = {q: f[q] - f[q + 1] for q in range(1, Q, 2)}
    pxx = s[1] + s[7] + s[9] + s[11] + s[13]
    pyy = s[3] + s[7] + s[9] + s[15] + s[17]
    pzz = s[5] + s[11] + s[13] + s[15] + s[17]
    pxy = s[7] - s[9]
    pxz = s[11] - s[13]
    pyz = s[15] - s[17]
    rho = f[0] + s[1] + s[3] + s[5] + s[7] + s[9] + s[11] + s[13] + s[15] + s[17]
    inv_rho = 1.0 / rho
    ux = (d[1] + d[7] + d[9] + d[11] + d[13]) * inv_rho
    uy = (d[3] + d[7] - d[9] + d[15] + d[17]) * inv_rho
    uz = (d[5] + d[11] - d[13] + d[15] - d[17]) * inv_rho
    third = rho * (1.0 / 3.0)
    sxx = pxx - third - rho * ux * ux
    syy = pyy - third - rho * uy * uy
    szz = pzz - third - rho * uz * uz
    sxy = pxy - rho * ux * uy
    sxz = pxz - rho * ux * uz
    syz = pyz - rho * uy * uz
    contracted = sxx * sxx + syy * syy + szz * szz + 2.0 * (sxy * sxy + sxz * sxz + syz * syz)
    rate = 1.5 / 0.8 * inv_rho * jnp.sqrt(2.0 * contracted)
    scaled = 20.0 * rate
    viscosity = 0.01 + 0.09 * lax.rsqrt(jnp.sqrt(1.0 + scaled * scaled))
    omega = 1.0 / (3.0 * viscosity + 0.5)
    speed = 1.0 - 1.5 * (ux * ux + uy * uy + uz * uz)
    vel = (ux, uy, uz)
    out = [None] * Q
    out[0] = f[0] - (f[0] - WTS[0] * rho * speed) * omega
    for q in range(1, Q, 2):
        proj = None
        for comp, step in zip(vel, (CX[q], CY[q], CZ[q])):
            if step:
                term = comp if step > 0 else -comp
                proj = term if proj is None else proj + term
        scale = WTS[q] * rho
        even = scale * (speed + 4.5 * proj * proj)
        odd = scale * (3.0 * proj)
        out[q] = f[q] - (f[q] - (even + odd)) * omega
        out[q + 1] = f[q + 1] - (f[q + 1] - (even - odd)) * omega
    return out


def first_kernel(pdf_ref, grains_ref, moves_ref, col_ref, up_ref, dn_ref):
    lane = iota((ROWS, LANE), 1)
    col = collide([pdf_ref[q] for q in range(Q)])
    for q in range(Q):
        col_ref[q] = col[q]
    for ref, chosen, edge in ((up_ref, YUP, LANE - Z), (dn_ref, YDN, 0)):
        rim = jnp.zeros((ROWS, LANE), F32)
        for k, q in enumerate(chosen):
            moved = pltpu.roll(z_shift(col[q], CZ[q], lane), (k * Z - edge) % LANE, 1)
            rim = jnp.where(lane // Z == k, moved, rim)
        ref[0:ROWS, :] = rim
    moves = moves_ref[...]
    count = moves.shape[1]
    matches = (iota((16, count), 0) == moves).astype(F32)
    earlier = (iota((count, count), 0) < iota((count, count), 1)).astype(F32).astype(BF16)
    before = dot_nn(matches.astype(BF16), earlier)
    rank = jnp.sum(matches * before, axis=0, keepdims=True).astype(I32)
    region = jnp.where(moves > 4, moves - 1, moves)
    target = jnp.where(moves == 4, -1, region * 8 + rank)
    placing = (iota((LANE, count), 0) == target).astype(F32).astype(BF16)
    own = grains_ref[:, 0, :]
    high, middle, low = split3(own)
    packed = dot_nt(high, placing) + dot_nt(middle, placing) + dot_nt(low, placing)
    for ref in (up_ref, dn_ref):
        ref[ROWS : ROWS + GV, :] = packed
        ref[ROWS + GV :, :] = jnp.zeros((6, LANE), F32)


def y_shifted(q, plane, ylo, yhi, lane):
    plane = z_shift(plane, CZ[q], lane)
    if CY[q] == 1:
        k = YUP.index(q)
        return jnp.where(lane < Z, pltpu.roll(ylo, (LANE - k * Z) % LANE, 1), pltpu.roll(plane, Z, 1))
    if CY[q] == -1:
        k = YDN.index(q)
        return jnp.where(
            lane >= LANE - Z,
            pltpu.roll(yhi, (LANE - Z - k * Z) % LANE, 1),
            pltpu.roll(plane, LANE - Z, 1),
        )
    return plane


def second_kernel(col_ref, mine_ref, ylo_ref, yhi_ref, up_ref, dn_ref):
    lane = iota((8, LANE), 1)
    for ref, chosen, part, row in ((up_ref, XUP, 8, 7), (dn_ref, XDN, 0, 0)):
        ref[0:8, :] = jnp.zeros((8, LANE), F32)
        ylo = ylo_ref[part : part + 8, :]
        yhi = yhi_ref[part : part + 8, :]
        for k, q in enumerate(chosen):
            shifted = y_shifted(q, col_ref[q, part : part + 8, :], ylo, yhi, lane)
            ref[k : k + 1, :] = shifted[row : row + 1, :]
    grain_lane = iota((32, LANE), 1) // 8
    joined = jnp.where(
        one_of(grain_lane, (2, 4, 7)),
        ylo_ref[ROWS:, :],
        jnp.where(one_of(grain_lane, (0, 3, 5)), yhi_ref[ROWS:, :], mine_ref[ROWS:, :]),
    )
    up_ref[8:, :] = joined
    dn_ref[8:, :] = joined


def link_terms(cell, direction, picked, block_x, block_y):
    def component(table):
        plus = one_of(direction, [q for q in range(Q) if table[q] == 1])
        minus = one_of(direction, [q for q in range(Q) if table[q] == -1])
        return jnp.where(plus, 1.0, jnp.where(minus, -1.0, 0.0))

    step_x, step_y, step_z = component(CX), component(CY), component(CZ)
    scale = jnp.where(direction <= 6, W6_AXIS, W6_DIAG)
    rel_x = (block_x * E + cell // (E * Z)).astype(F32) + 0.5 * step_x - picked[0:1]
    rel_y = (block_y * E + cell // Z % E).astype(F32) + 0.5 * step_y - picked[1:2]
    rel_z = (cell % Z).astype(F32) + 0.5 * step_z - picked[2:3]
    wall_x = picked[3:4] + picked[7:8] * rel_z - picked[8:9] * rel_y
    wall_y = picked[4:5] + picked[8:9] * rel_x - picked[6:7] * rel_z
    wall_z = picked[5:6] + picked[6:7] * rel_y - picked[7:8] * rel_x
    return scale * (step_x * wall_x + step_y * wall_y + step_z * wall_z)


def third_kernel(
    place_ref, owner_ref, col_ref, ylo_ref, yhi_ref, mine_ref, xlo_ref, xhi_ref, grains_ref, moves_ref,
    link_ref, send_ref, table_ref, final_ref, block_ref,
):
    lane = iota((ROWS, LANE), 1)
    row = iota((ROWS, LANE), 0)
    grain_lane = iota((32, LANE), 1) // 8
    arrived = jnp.where(
        one_of(grain_lane, (5, 6, 7)),
        xlo_ref[8:, :],
        jnp.where(one_of(grain_lane, (0, 1, 2)), xhi_ref[8:, :], mine_ref[8:, :]),
    )
    own = grains_ref[:, 0, :]
    kept = jnp.where(moves_ref[...] == 4, own, 0.0)
    table_ref[:, 0, 0:256] = kept
    table_ref[:, 0, 256:320] = arrived[0:GV, 0:64]
    kept_parts = jnp.concatenate(split3(kept[0:16]), axis=0)
    arrived_parts = jnp.concatenate(split3(arrived[0:16]), axis=0)
    corrections = []
    directions = []
    for bx in range(2):
        cell = link_ref[0, bx : bx + 1, :]
        direction = link_ref[1, bx : bx + 1, :]
        slot = link_ref[2, bx : bx + 1, :]
        links = cell.shape[1]
        pick_kept = (iota((256, links), 0) == slot).astype(F32).astype(BF16)
        pick_arrived = (iota((LANE, links), 0) + 256 == slot).astype(F32).astype(BF16)
        picked = dot_nn(kept_parts, pick_kept) + dot_nn(arrived_parts, pick_arrived)
        picked = picked[0:16] + picked[16:32] + picked[32:48]
        side = iota((1, links), 1) // 256
        correction = link_terms(cell, direction, picked, place_ref[0] * 2 + bx, place_ref[1] * 2 + side)
        at_row = iota((8, links), 0) == cell // 64
        values = [part.astype(F32) for part in split3(correction)] + [direction.astype(F32)]
        left = jnp.concatenate([jnp.where(at_row, value, 0.0) for value in values], axis=0).astype(BF16)
        right = (iota((LANE, links), 0) == side * 64 + cell % 64).astype(F32).astype(BF16)
        dense = dot_nt(left, right)
        corrections.append(dense[0:8] + dense[8:16] + dense[16:24])
        directions.append(dense[24:32])
    correction = jnp.concatenate(corrections, axis=0)
    direction = jnp.concatenate(directions, axis=0).astype(I32)
    ylo = ylo_ref[0:ROWS, :]
    yhi = yhi_ref[0:ROWS, :]
    for q in range(Q):
        plane = y_shifted(q, col_ref[q], ylo, yhi, lane)
        if CX[q] == 1:
            k = XUP.index(q)
            plane = jnp.where(row == 0, xlo_ref[k : k + 1, :], pltpu.roll(plane, 1, 0))
        elif CX[q] == -1:
            k = XDN.index(q)
            plane = jnp.where(row == ROWS - 1, xhi_ref[k : k + 1, :], pltpu.roll(plane, ROWS - 1, 0))
        if q:
            plane = jnp.where(direction == OPP[q], col_ref[OPP[q]] - correction, plane)
        final_ref[q] = plane
    low_half = iota((8, LANE), 1) < 64
    for q in range(Q):
        even = final_ref[q, pl.ds(0, 8, stride=2), :]
        odd = final_ref[q, pl.ds(1, 8, stride=2), :]
        first = jnp.where(low_half, even, pltpu.roll(odd, 64, 1))
        second = jnp.where(low_half, pltpu.roll(even, 64, 1), odd)
        for bx in range(2):
            block_ref[bx * 2, 4 * q : 4 * q + 4, :] = first[4 * bx : 4 * bx + 4]
            block_ref[bx * 2 + 1, 4 * q : 4 * q + 4, :] = second[4 * bx : 4 * bx + 4]
    send_ref[...] = jnp.zeros(send_ref.shape, F32)
    for n in range(4):
        send_ref[owner_ref[n // 2, n % 2]] = block_ref[n]


def last_kernel(got_ref, out_ref):
    for slot in range(got_ref.shape[0]):
        out_ref[76 * slot : 76 * slot + 76, :] = got_ref[slot]


VMEM = pl.BlockSpec(memory_space=pltpu.VMEM)
SMEM = pl.BlockSpec(memory_space=pltpu.SMEM)


def ring(axis, step):
    count = lax.axis_size(axis)
    return [(i, (i + step) % count) for i in range(count)]


def body(pdf, grains, grain_moves, owner_map, link_lists):
    group = lax.axis_size("gx")
    place = jnp.stack([lax.axis_index("gx"), lax.axis_index("gy")]).astype(I32)

    def shape(*dims):
        return jax.ShapeDtypeStruct(dims, F32)

    col, y_up, y_dn = pl.pallas_call(
        first_kernel,
        out_shape=(shape(Q, ROWS, LANE), shape(48, LANE), shape(48, LANE)),
        in_specs=[VMEM] * 3,
        out_specs=(VMEM,) * 3,
        name="collide_pack",
    )(pdf, grains, grain_moves)
    ylo = lax.ppermute(y_up, "gy", ring("gy", 1))
    yhi = lax.ppermute(y_dn, "gy", ring("gy", -1))
    x_up, x_dn = pl.pallas_call(
        second_kernel,
        out_shape=(shape(40, LANE), shape(40, LANE)),
        in_specs=[VMEM] * 4,
        out_specs=(VMEM,) * 2,
        name="x_messages",
    )(col, y_up, ylo, yhi)
    xlo = lax.ppermute(x_up, "gx", ring("gx", 1))
    xhi = lax.ppermute(x_dn, "gx", ring("gx", -1))
    send, table = pl.pallas_call(
        third_kernel,
        out_shape=(shape(group, 76, LANE), shape(GV, 1, 320)),
        in_specs=[SMEM, SMEM] + [VMEM] * 9,
        out_specs=(VMEM,) * 2,
        scratch_shapes=[pltpu.VMEM((Q, ROWS, LANE), F32), pltpu.VMEM((4, 76, LANE), F32)],
        name="finish_blocks",
    )(place, owner_map, col, ylo, yhi, x_up, xlo, xhi, grains, grain_moves, link_lists)
    got = lax.all_to_all(send, "gx", split_axis=0, concat_axis=0, tiled=True)
    out = pl.pallas_call(
        last_kernel,
        out_shape=shape(group * 76, LANE),
        in_specs=[VMEM],
        out_specs=VMEM,
        name="lay_out",
    )(got)
    return (out.reshape(group, 1, Q, 512), table)


def solution(mesh):
    in_specs = (
        P(None, "gx", "gy"),
        P(None, "gx", "gy"),
        P("gx", "gy"),
        P("gx", "gy"),
        P(None, "gx", "gy"),
    )
    out_specs = (P("gx", "gy", None, None), P(None, "gx", "gy"))
    return jax.shard_map(body, mesh=mesh, in_specs=in_specs, out_specs=out_specs, check_vma=False)
```

```python
import jax
import jax.numpy as jnp
import numpy as np
from jax import lax
from jax.experimental import pallas as pl
from jax.experimental.pallas import tpu as pltpu
from jax.sharding import PartitionSpec as P

Q = 19
E = 8
Z = 8
ROWS = 16
LANE = 128
GV = 26

CX = (0, 1, -1, 0, 0, 0, 0, 1, -1, 1, -1, 1, -1, 1, -1, 0, 0, 0, 0)
CY = (0, 0, 0, 1, -1, 0, 0, 1, -1, -1, 1, 0, 0, 0, 0, 1, -1, 1, -1)
CZ = (0, 0, 0, 0, 0, 1, -1, 0, 0, 0, 0, 1, -1, -1, 1, 1, -1, -1, 1)
OPP = (0, 2, 1, 4, 3, 6, 5, 8, 7, 10, 9, 12, 11, 14, 13, 16, 15, 18, 17)
WTS = tuple(float(np.float32(w)) for w in [1.0 / 3.0] + [1.0 / 18.0] * 6 + [1.0 / 36.0] * 12)
W6_AXIS = float(np.float32(6.0) * np.float32(1.0 / 18.0))
W6_DIAG = float(np.float32(6.0) * np.float32(1.0 / 36.0))
XUP = tuple(q for q in range(Q) if CX[q] == 1)
XDN = tuple(q for q in range(Q) if CX[q] == -1)
YUP = tuple(q for q in range(Q) if CY[q] == 1)
YDN = tuple(q for q in range(Q) if CY[q] == -1)
CODES = (0, 1, 2, 3, 5, 6, 7, 8)

F32 = jnp.float32
BF16 = jnp.bfloat16
I32 = jnp.int32


def iota(shape, dim):
    return lax.broadcasted_iota(I32, shape, dim)


def split3(value):
    high = value.astype(BF16)
    rest = value - high.astype(F32)
    middle = rest.astype(BF16)
    low = (rest - middle.astype(F32)).astype(BF16)
    return high, middle, low


def dot_nt(a, b):
    return lax.dot_general(a, b, (((1,), (1,)), ((), ())), preferred_element_type=F32)


def dot_nn(a, b):
    return lax.dot_general(a, b, (((1,), (0,)), ((), ())), preferred_element_type=F32)


def one_of(index, chosen):
    hit = index == chosen[0]
    for value in chosen[1:]:
        hit = jnp.logical_or(hit, index == value)
    return hit


def z_shift(plane, step, lane):
    depth = lane % Z
    if step == 1:
        return jnp.where(depth == 0, pltpu.roll(plane, LANE - (Z - 1), 1), pltpu.roll(plane, 1, 1))
    if step == -1:
        return jnp.where(depth == Z - 1, pltpu.roll(plane, Z - 1, 1), pltpu.roll(plane, LANE - 1, 1))
    return plane


def collide(f):
    s = {q: f[q] + f[q + 1] for q in range(1, Q, 2)}
    d = {q: f[q] - f[q + 1] for q in range(1, Q, 2)}
    pxx = s[1] + s[7] + s[9] + s[11] + s[13]
    pyy = s[3] + s[7] + s[9] + s[15] + s[17]
    pzz = s[5] + s[11] + s[13] + s[15] + s[17]
    pxy = s[7] - s[9]
    pxz = s[11] - s[13]
    pyz = s[15] - s[17]
    rho = f[0] + s[1] + s[3] + s[5] + s[7] + s[9] + s[11] + s[13] + s[15] + s[17]
    inv_rho = 1.0 / rho
    ux = (d[1] + d[7] + d[9] + d[11] + d[13]) * inv_rho
    uy = (d[3] + d[7] - d[9] + d[15] + d[17]) * inv_rho
    uz = (d[5] + d[11] - d[13] + d[15] - d[17]) * inv_rho
    third = rho * (1.0 / 3.0)
    sxx = pxx - third - rho * ux * ux
    syy = pyy - third - rho * uy * uy
    szz = pzz - third - rho * uz * uz
    sxy = pxy - rho * ux * uy
    sxz = pxz - rho * ux * uz
    syz = pyz - rho * uy * uz
    contracted = sxx * sxx + syy * syy + szz * szz + 2.0 * (sxy * sxy + sxz * sxz + syz * syz)
    rate = 1.5 / 0.8 * inv_rho * jnp.sqrt(2.0 * contracted)
    scaled = 20.0 * rate
    viscosity = 0.01 + 0.09 * lax.rsqrt(jnp.sqrt(1.0 + scaled * scaled))
    omega = 1.0 / (3.0 * viscosity + 0.5)
    speed = 1.0 - 1.5 * (ux * ux + uy * uy + uz * uz)
    vel = (ux, uy, uz)
    out = [None] * Q
    out[0] = f[0] - (f[0] - WTS[0] * rho * speed) * omega
    for q in range(1, Q, 2):
        proj = None
        for comp, step in zip(vel, (CX[q], CY[q], CZ[q])):
            if step:
                term = comp if step > 0 else -comp
                proj = term if proj is None else proj + term
        scale = WTS[q] * rho
        even = scale * (speed + 4.5 * proj * proj)
        odd = scale * (3.0 * proj)
        out[q] = f[q] - (f[q] - (even + odd)) * omega
        out[q + 1] = f[q + 1] - (f[q + 1] - (even - odd)) * omega
    return out


def first_kernel(pdf_ref, grains_ref, moves_ref, col_ref, up_ref, dn_ref):
    lane = iota((ROWS, LANE), 1)
    col = collide([pdf_ref[q] for q in range(Q)])
    for q in range(Q):
        col_ref[q] = col[q]
    for ref, chosen, edge in ((up_ref, YUP, LANE - Z), (dn_ref, YDN, 0)):
        rim = jnp.zeros((ROWS, LANE), F32)
        for k, q in enumerate(chosen):
            moved = pltpu.roll(z_shift(col[q], CZ[q], lane), (k * Z - edge) % LANE, 1)
            rim = jnp.where(lane // Z == k, moved, rim)
        ref[0:ROWS, :] = rim
    moves = moves_ref[...]
    count = moves.shape[1]
    matches = (iota((16, count), 0) == moves).astype(F32)
    earlier = (iota((count, count), 0) < iota((count, count), 1)).astype(F32).astype(BF16)
    before = dot_nn(matches.astype(BF16), earlier)
    rank = jnp.sum(matches * before, axis=0, keepdims=True).astype(I32)
    region = jnp.where(moves > 4, moves - 1, moves)
    target = jnp.where(moves == 4, -1, region * 8 + rank)
    placing = (iota((LANE, count), 0) == target).astype(F32).astype(BF16)
    own = grains_ref[:, 0, :]
    high, middle, low = split3(own)
    packed = dot_nt(high, placing) + dot_nt(middle, placing) + dot_nt(low, placing)
    for ref in (up_ref, dn_ref):
        ref[ROWS : ROWS + GV, :] = packed
        ref[ROWS + GV :, :] = jnp.zeros((6, LANE), F32)


def y_shifted(q, plane, ylo, yhi, lane):
    plane = z_shift(plane, CZ[q], lane)
    if CY[q] == 1:
        k = YUP.index(q)
        return jnp.where(lane < Z, pltpu.roll(ylo, (LANE - k * Z) % LANE, 1), pltpu.roll(plane, Z, 1))
    if CY[q] == -1:
        k = YDN.index(q)
        return jnp.where(
            lane >= LANE - Z,
            pltpu.roll(yhi, (LANE - Z - k * Z) % LANE, 1),
            pltpu.roll(plane, LANE - Z, 1),
        )
    return plane


def second_kernel(col_ref, mine_ref, ylo_ref, yhi_ref, after_ref, up_ref, dn_ref):
    del after_ref
    lane = iota((8, LANE), 1)
    for ref, chosen, part, row in ((up_ref, XUP, 8, 7), (dn_ref, XDN, 0, 0)):
        ref[0:8, :] = jnp.zeros((8, LANE), F32)
        ylo = ylo_ref[part : part + 8, :]
        yhi = yhi_ref[part : part + 8, :]
        for k, q in enumerate(chosen):
            shifted = y_shifted(q, col_ref[q, part : part + 8, :], ylo, yhi, lane)
            ref[k : k + 1, :] = shifted[row : row + 1, :]
    grain_lane = iota((32, LANE), 1) // 8
    joined = jnp.where(
        one_of(grain_lane, (2, 4, 7)),
        ylo_ref[ROWS:, :],
        jnp.where(one_of(grain_lane, (0, 3, 5)), yhi_ref[ROWS:, :], mine_ref[ROWS:, :]),
    )
    up_ref[8:, :] = joined
    dn_ref[8:, :] = joined


def link_kernel(place_x_ref, place_y_ref, link_ref, after_ref, kept_ref, arrived_ref, spread_ref, term_ref, dense_ref):
    del after_ref
    for bx in range(2):
        cell = link_ref[0, bx : bx + 1, :]
        direction = link_ref[1, bx : bx + 1, :]
        slot = link_ref[2, bx : bx + 1, :]
        links = cell.shape[1]
        side = iota((1, links), 1) // 256

        def component(table):
            plus = one_of(direction, [q for q in range(Q) if table[q] == 1])
            minus = one_of(direction, [q for q in range(Q) if table[q] == -1])
            return jnp.where(plus, 1.0, jnp.where(minus, -1.0, 0.0))

        steps = [component(table) for table in (CX, CY, CZ)]
        corner = (
            (place_x_ref[0] * 2 + bx) * E + cell // (E * Z),
            (place_y_ref[0] * 2 + side) * E + cell // Z % E,
            cell % Z,
        )
        row = cell // (E * Z)
        terms = [c.astype(F32) + 0.5 * step for c, step in zip(corner, steps)] + steps
        terms += [jnp.where(direction <= 6, W6_AXIS, W6_DIAG), row.astype(F32)]
        for k, term in enumerate(terms):
            term_ref[bx, k : k + 1, :] = term
        kept_ref[bx] = (iota((256, links), 0) == slot).astype(F32).astype(BF16)
        arrived_ref[bx] = (iota((LANE, links), 0) + 256 == slot).astype(F32).astype(BF16)
        spread = (iota((LANE, links), 0) == side * 64 + cell % 64).astype(F32).astype(BF16)
        spread_ref[bx] = spread
        left = jnp.where(iota((8, links), 0) == row, direction.astype(F32), 0.0).astype(BF16)
        dense_ref[8 * bx : 8 * bx + 8, :] = dot_nt(left, spread)


def block_order(scratch_ref, plane):
    low_half = iota((8, LANE), 1) < 64
    scratch_ref[...] = plane
    even = scratch_ref[pl.ds(0, 8, stride=2), :]
    odd = scratch_ref[pl.ds(1, 8, stride=2), :]
    first = jnp.where(low_half, even, pltpu.roll(odd, 64, 1))
    second = jnp.where(low_half, pltpu.roll(even, 64, 1), odd)
    return first, second


def shift_kernel(
    col_ref, ylo_ref, yhi_ref, mine_ref, grains_ref, moves_ref, kept_ref, arrived_ref, dense_ref, after_ref,
    plane_ref, value_ref, toward_ref, pick_ref, own_ref, scratch_ref,
):
    del after_ref
    lane = iota((ROWS, LANE), 1)
    ylo = ylo_ref[0:ROWS, :]
    yhi = yhi_ref[0:ROWS, :]
    for q in range(Q):
        plane = y_shifted(q, col_ref[q], ylo, yhi, lane)
        if CX[q]:
            plane = pltpu.roll(plane, CX[q] % ROWS, 0)
        for ref, given in ((plane_ref, plane), (value_ref, col_ref[OPP[q]])):
            for half, part in enumerate(block_order(scratch_ref.at[q % 4 + (4 if ref is value_ref else 0)], given)):
                ref[q, half] = part
    for half, part in enumerate(block_order(scratch_ref.at[0], dense_ref[...])):
        toward_ref[half] = part.astype(I32)
    kept = jnp.where(moves_ref[...] == 4, grains_ref[:, 0, :], 0.0)
    own_ref[...] = kept
    stay = one_of(iota((32, LANE), 1) // 8, (3, 4))
    arrived = jnp.where(stay, mine_ref[8:, :], 0.0)
    kept_parts = jnp.concatenate(split3(kept[0:16]), axis=0)
    arrived_parts = jnp.concatenate(split3(arrived[0:16]), axis=0)
    for bx in range(2):
        picked = dot_nn(kept_parts, kept_ref[bx]) + dot_nn(arrived_parts, arrived_ref[bx])
        pick_ref[bx] = picked[0:16] + picked[16:32] + picked[32:48]


def table_kernel(mine_ref, xlo_ref, xhi_ref, own_ref, table_ref):
    grain_lane = iota((32, LANE), 1) // 8
    arrived = jnp.where(
        one_of(grain_lane, (5, 6, 7)),
        xlo_ref[8:, :],
        jnp.where(one_of(grain_lane, (0, 1, 2)), xhi_ref[8:, :], mine_ref[8:, :]),
    )
    table_ref[:, 0, 0:256] = own_ref[...]
    table_ref[:, 0, 256:320] = arrived[0:GV, 0:64]


def finish_kernel(
    owner_ref, plane_ref, value_ref, toward_ref, xlo_ref, xhi_ref, pick_ref,
    arrived_ref, spread_ref, term_ref, send_ref, scratch_ref,
):
    send_ref[...] = jnp.zeros(send_ref.shape, F32)
    grain_lane = iota((16, LANE), 1) // 8
    moved = jnp.where(
        one_of(grain_lane, (5, 6, 7)),
        xlo_ref[8:24, :],
        jnp.where(one_of(grain_lane, (0, 1, 2)), xhi_ref[8:24, :], 0.0),
    )
    moved_parts = jnp.concatenate(split3(moved), axis=0)
    corrections = []
    for bx in range(2):
        picked = dot_nn(moved_parts, arrived_ref[bx])
        g = pick_ref[bx] + (picked[0:16] + picked[16:32] + picked[32:48])
        mid_x, mid_y, mid_z, step_x, step_y, step_z, scale, at = (term_ref[bx, k : k + 1, :] for k in range(8))
        rel_x = mid_x - g[0:1]
        rel_y = mid_y - g[1:2]
        rel_z = mid_z - g[2:3]
        wall_x = g[3:4] + g[7:8] * rel_z - g[8:9] * rel_y
        wall_y = g[4:5] + g[8:9] * rel_x - g[6:7] * rel_z
        wall_z = g[5:6] + g[6:7] * rel_y - g[7:8] * rel_x
        correction = scale * (step_x * wall_x + step_y * wall_y + step_z * wall_z)
        here = iota((8, correction.shape[1]), 0) == at.astype(I32)
        left = jnp.concatenate(
            [jnp.where(here, part.astype(F32), 0.0) for part in split3(correction)], axis=0
        ).astype(BF16)
        dense = dot_nt(left, spread_ref[bx])
        corrections.append(dense[0:8] + dense[8:16] + dense[16:24])
    correction = jnp.concatenate(corrections, axis=0)
    correction = block_order(scratch_ref, correction)
    base = [owner_ref[n // 2, n % 2] * Q for n in range(4)]
    low_half = iota((8, LANE), 1) < 64
    row = iota((8, LANE), 0)
    first_row = jnp.logical_and(row == 0, low_half)
    last_row = jnp.logical_and(row == 7, jnp.logical_not(low_half))
    turned_low = pltpu.roll(xlo_ref[0:8, :], 64, 1)
    turned_high = pltpu.roll(xhi_ref[0:8, :], 64, 1)
    for q in range(Q):
        for half in range(2):
            part = plane_ref[q, half]
            if CX[q] == 1:
                k = XUP.index(q)
                edge = turned_low[k : k + 1] if half else xlo_ref[k : k + 1, :]
                part = jnp.where(first_row, edge, part)
            elif CX[q] == -1:
                k = XDN.index(q)
                edge = xhi_ref[k : k + 1, :] if half else turned_high[k : k + 1]
                part = jnp.where(last_row, edge, part)
            if q:
                part = jnp.where(toward_ref[half] == OPP[q], value_ref[q, half] - correction[half], part)
            send_ref[base[half] + q] = part[0:4]
            send_ref[base[2 + half] + q] = part[4:8]


VMEM = pl.BlockSpec(memory_space=pltpu.VMEM)
SMEM = pl.BlockSpec(memory_space=pltpu.SMEM)


def ring(axis, step):
    count = lax.axis_size(axis)
    return [(i, (i + step) % count) for i in range(count)]


def near(*arrays):
    return tuple(pltpu.with_memory_space_constraint(a, pltpu.VMEM) for a in arrays)


def chip(*dims, dtype=F32):
    return pltpu.VMEM(dims, dtype)


def body(pdf, grains, grain_moves, owner_map, link_lists):
    group = lax.axis_size("gx")
    place_x = lax.axis_index("gx").astype(I32).reshape(1)
    place_y = lax.axis_index("gy").astype(I32).reshape(1)
    links = link_lists.shape[2]
    col, y_up, y_dn = pl.pallas_call(
        first_kernel,
        out_shape=(chip(Q, ROWS, LANE), chip(48, LANE), chip(48, LANE)),
        in_specs=[VMEM] * 3,
        out_specs=(VMEM,) * 3,
        name="collide_pack",
    )(pdf, grains, grain_moves)
    ylo = lax.ppermute(y_up, "gy", ring("gy", 1))
    yhi = lax.ppermute(y_dn, "gy", ring("gy", -1))
    kept, arrived, spread, terms, dense = pl.pallas_call(
        link_kernel,
        out_shape=(
            chip(2, 256, links, dtype=BF16),
            chip(2, LANE, links, dtype=BF16),
            chip(2, LANE, links, dtype=BF16),
            chip(2, 8, links),
            chip(ROWS, LANE),
        ),
        in_specs=[SMEM, SMEM, VMEM, VMEM],
        out_specs=(VMEM,) * 5,
        cost_estimate=pl.CostEstimate(flops=4_000_000, bytes_accessed=1_000_000, transcendentals=0),
        name="link_maps",
    )(place_x, place_y, link_lists, *near(y_up))
    x_up, x_dn = pl.pallas_call(
        second_kernel,
        out_shape=(chip(40, LANE), chip(40, LANE)),
        in_specs=[VMEM] * 5,
        out_specs=(VMEM,) * 2,
        name="x_messages",
    )(*near(col, y_up, ylo, yhi, terms))
    xlo = lax.ppermute(x_up, "gx", ring("gx", 1))
    xhi = lax.ppermute(x_dn, "gx", ring("gx", -1))
    plane, value, toward, pick, own = pl.pallas_call(
        shift_kernel,
        out_shape=(
            chip(Q, 2, 8, LANE),
            chip(Q, 2, 8, LANE),
            chip(2, 8, LANE, dtype=I32),
            chip(2, 16, links),
            chip(GV, 256),
        ),
        in_specs=[VMEM] * 10,
        out_specs=(VMEM,) * 5,
        scratch_shapes=[pltpu.VMEM((8, ROWS, LANE), F32)],
        cost_estimate=pl.CostEstimate(flops=4_000_000, bytes_accessed=1_000_000, transcendentals=0),
        name="shift_planes",
    )(*near(col, ylo, yhi, x_up), grains, grain_moves, *near(kept, arrived, dense, x_dn))
    send = pl.pallas_call(
        finish_kernel,
        out_shape=jax.ShapeDtypeStruct((group * Q, 4, LANE), F32),
        in_specs=[SMEM] + [VMEM] * 9,
        out_specs=VMEM,
        scratch_shapes=[pltpu.VMEM((ROWS, LANE), F32)],
        name="finish_blocks",
    )(owner_map, *near(plane, value, toward, xlo, xhi, pick, arrived, spread, terms))
    table = pl.pallas_call(
        table_kernel,
        out_shape=jax.ShapeDtypeStruct((GV, 1, 320), F32),
        in_specs=[VMEM] * 4,
        out_specs=VMEM,
        name="grain_table",
    )(*near(x_up, xlo, xhi, own))
    out = lax.all_to_all(send.reshape(group, 1, Q, 512), "gx", split_axis=0, concat_axis=0, tiled=True)
    return (out, table)


def solution(mesh):
    in_specs = (
        P(None, "gx", "gy"),
        P(None, "gx", "gy"),
        P("gx", "gy"),
        P("gx", "gy"),
        P(None, "gx", "gy"),
    )
    out_specs = (P("gx", "gy", None, None), P(None, "gx", "gy"))
    return jax.shard_map(body, mesh=mesh, in_specs=in_specs, out_specs=out_specs, check_vma=False)
```

```python
import jax
import jax.numpy as jnp
import numpy as np
from jax import lax
from jax.experimental import pallas as pl
from jax.experimental.pallas import tpu as pltpu
from jax.sharding import PartitionSpec as P

Q = 19
E = 8
Z = 8
ROWS = 16
LANE = 128
GV = 26

CX = (0, 1, -1, 0, 0, 0, 0, 1, -1, 1, -1, 1, -1, 1, -1, 0, 0, 0, 0)
CY = (0, 0, 0, 1, -1, 0, 0, 1, -1, -1, 1, 0, 0, 0, 0, 1, -1, 1, -1)
CZ = (0, 0, 0, 0, 0, 1, -1, 0, 0, 0, 0, 1, -1, -1, 1, 1, -1, -1, 1)
OPP = (0, 2, 1, 4, 3, 6, 5, 8, 7, 10, 9, 12, 11, 14, 13, 16, 15, 18, 17)
WTS = tuple(float(np.float32(w)) for w in [1.0 / 3.0] + [1.0 / 18.0] * 6 + [1.0 / 36.0] * 12)
W6_AXIS = float(np.float32(6.0) * np.float32(1.0 / 18.0))
W6_DIAG = float(np.float32(6.0) * np.float32(1.0 / 36.0))
XUP = tuple(q for q in range(Q) if CX[q] == 1)
XDN = tuple(q for q in range(Q) if CX[q] == -1)
YUP = tuple(q for q in range(Q) if CY[q] == 1)
YDN = tuple(q for q in range(Q) if CY[q] == -1)
CODES = (0, 1, 2, 3, 5, 6, 7, 8)

F32 = jnp.float32
BF16 = jnp.bfloat16
I32 = jnp.int32


def iota(shape, dim):
    return lax.broadcasted_iota(I32, shape, dim)


def split3(value):
    high = value.astype(BF16)
    rest = value - high.astype(F32)
    middle = rest.astype(BF16)
    low = (rest - middle.astype(F32)).astype(BF16)
    return high, middle, low


def dot_nt(a, b):
    return lax.dot_general(a, b, (((1,), (1,)), ((), ())), preferred_element_type=F32)


def dot_nn(a, b):
    return lax.dot_general(a, b, (((1,), (0,)), ((), ())), preferred_element_type=F32)


def one_of(index, chosen):
    hit = index == chosen[0]
    for value in chosen[1:]:
        hit = jnp.logical_or(hit, index == value)
    return hit


def z_shift(plane, step, lane):
    depth = lane % Z
    if step == 1:
        return jnp.where(depth == 0, pltpu.roll(plane, LANE - (Z - 1), 1), pltpu.roll(plane, 1, 1))
    if step == -1:
        return jnp.where(depth == Z - 1, pltpu.roll(plane, Z - 1, 1), pltpu.roll(plane, LANE - 1, 1))
    return plane


def collide(f):
    s = {q: f[q] + f[q + 1] for q in range(1, Q, 2)}
    d = {q: f[q] - f[q + 1] for q in range(1, Q, 2)}
    pxx = s[1] + s[7] + s[9] + s[11] + s[13]
    pyy = s[3] + s[7] + s[9] + s[15] + s[17]
    pzz = s[5] + s[11] + s[13] + s[15] + s[17]
    pxy = s[7] - s[9]
    pxz = s[11] - s[13]
    pyz = s[15] - s[17]
    rho = f[0] + s[1] + s[3] + s[5] + s[7] + s[9] + s[11] + s[13] + s[15] + s[17]
    inv_rho = 1.0 / rho
    ux = (d[1] + d[7] + d[9] + d[11] + d[13]) * inv_rho
    uy = (d[3] + d[7] - d[9] + d[15] + d[17]) * inv_rho
    uz = (d[5] + d[11] - d[13] + d[15] - d[17]) * inv_rho
    third = rho * (1.0 / 3.0)
    sxx = pxx - third - rho * ux * ux
    syy = pyy - third - rho * uy * uy
    szz = pzz - third - rho * uz * uz
    sxy = pxy - rho * ux * uy
    sxz = pxz - rho * ux * uz
    syz = pyz - rho * uy * uz
    contracted = sxx * sxx + syy * syy + szz * szz + 2.0 * (sxy * sxy + sxz * sxz + syz * syz)
    rate = 1.5 / 0.8 * inv_rho * jnp.sqrt(2.0 * contracted)
    scaled = 20.0 * rate
    viscosity = 0.01 + 0.09 * lax.rsqrt(jnp.sqrt(1.0 + scaled * scaled))
    omega = 1.0 / (3.0 * viscosity + 0.5)
    speed = 1.0 - 1.5 * (ux * ux + uy * uy + uz * uz)
    vel = (ux, uy, uz)
    out = [None] * Q
    out[0] = f[0] - (f[0] - WTS[0] * rho * speed) * omega
    for q in range(1, Q, 2):
        proj = None
        for comp, step in zip(vel, (CX[q], CY[q], CZ[q])):
            if step:
                term = comp if step > 0 else -comp
                proj = term if proj is None else proj + term
        scale = WTS[q] * rho
        even = scale * (speed + 4.5 * proj * proj)
        odd = scale * (3.0 * proj)
        out[q] = f[q] - (f[q] - (even + odd)) * omega
        out[q + 1] = f[q + 1] - (f[q + 1] - (even - odd)) * omega
    return out


def first_kernel(place_y_ref, pdf_ref, grains_ref, moves_ref, col_ref, near_ref, far_ref):
    lane = iota((ROWS, LANE), 1)
    col = collide([pdf_ref[q] for q in range(Q)])
    for q in range(Q):
        col_ref[q] = col[q]
    rims = []
    for chosen, edge in ((YUP, LANE - Z), (YDN, 0)):
        rim = jnp.zeros((ROWS, LANE), F32)
        for k, q in enumerate(chosen):
            moved = pltpu.roll(z_shift(col[q], CZ[q], lane), (k * Z - edge) % LANE, 1)
            rim = jnp.where(lane // Z == k, moved, rim)
        rims.append(rim)
    left = place_y_ref[0] % 2 == 0
    near_ref[0:ROWS, :] = jnp.where(left, rims[0], rims[1])
    far_ref[0:ROWS, :] = jnp.where(left, rims[1], rims[0])
    moves = moves_ref[...]
    count = moves.shape[1]
    matches = (iota((16, count), 0) == moves).astype(F32)
    earlier = (iota((count, count), 0) < iota((count, count), 1)).astype(F32).astype(BF16)
    before = dot_nn(matches.astype(BF16), earlier)
    rank = jnp.sum(matches * before, axis=0, keepdims=True).astype(I32)
    region = jnp.where(moves > 4, moves - 1, moves)
    target = jnp.where(moves == 4, -1, region * 8 + rank)
    placing = (iota((LANE, count), 0) == target).astype(F32).astype(BF16)
    own = grains_ref[:, 0, :]
    high, middle, low = split3(own)
    packed = dot_nt(high, placing) + dot_nt(middle, placing) + dot_nt(low, placing)
    for ref in (near_ref, far_ref):
        ref[ROWS : ROWS + GV, :] = packed
        ref[ROWS + GV :, :] = jnp.zeros((6, LANE), F32)


def y_shifted(q, plane, ylo, yhi, lane):
    plane = z_shift(plane, CZ[q], lane)
    if CY[q] == 1:
        k = YUP.index(q)
        return jnp.where(lane < Z, pltpu.roll(ylo, (LANE - k * Z) % LANE, 1), pltpu.roll(plane, Z, 1))
    if CY[q] == -1:
        k = YDN.index(q)
        return jnp.where(
            lane >= LANE - Z,
            pltpu.roll(yhi, (LANE - Z - k * Z) % LANE, 1),
            pltpu.roll(plane, LANE - Z, 1),
        )
    return plane


def from_pairs(place_y_ref, near_ref, far_ref, start, size):
    left = place_y_ref[0] % 2 == 0
    low = slice(start, start + size)
    high = slice(48 + start, 48 + start + size)
    ylo = jnp.where(left, far_ref[low, :], near_ref[low, :])
    yhi = jnp.where(left, near_ref[high, :], far_ref[high, :])
    return ylo, yhi


def second_kernel(place_y_ref, col_ref, mine_ref, near_ref, far_ref, up_ref, dn_ref):
    lane = iota((8, LANE), 1)
    for ref, chosen, part, row in ((up_ref, XUP, 8, 7), (dn_ref, XDN, 0, 0)):
        ref[0:8, :] = jnp.zeros((8, LANE), F32)
        ylo, yhi = from_pairs(place_y_ref, near_ref, far_ref, part, 8)
        for k, q in enumerate(chosen):
            shifted = y_shifted(q, col_ref[q, part : part + 8, :], ylo, yhi, lane)
            ref[k : k + 1, :] = shifted[row : row + 1, :]
    grain_lane = iota((32, LANE), 1) // 8
    ylo, yhi = from_pairs(place_y_ref, near_ref, far_ref, ROWS, 32)
    joined = jnp.where(
        one_of(grain_lane, (2, 4, 7)), ylo, jnp.where(one_of(grain_lane, (0, 3, 5)), yhi, mine_ref[ROWS:, :])
    )
    up_ref[8:, :] = joined
    dn_ref[8:, :] = joined


def link_maps(place_x_ref, place_y_ref, link_ref, kept_parts, stay_parts, arrived_ref, spread_ref, term_ref, pick_ref):
    toward = []
    for bx in range(2):
        cell = link_ref[0, bx : bx + 1, :]
        direction = link_ref[1, bx : bx + 1, :]
        slot = link_ref[2, bx : bx + 1, :]
        links = cell.shape[1]
        side = iota((1, links), 1) // 256

        def component(table):
            plus = one_of(direction, [q for q in range(Q) if table[q] == 1])
            minus = one_of(direction, [q for q in range(Q) if table[q] == -1])
            return jnp.where(plus, 1.0, jnp.where(minus, -1.0, 0.0))

        steps = [component(table) for table in (CX, CY, CZ)]
        corner = (
            (place_x_ref[0] * 2 + bx) * E + cell // (E * Z),
            (place_y_ref[0] * 2 + side) * E + cell // Z % E,
            cell % Z,
        )
        row = cell // (E * Z)
        terms = [c.astype(F32) + 0.5 * step for c, step in zip(corner, steps)] + steps
        terms += [jnp.where(direction <= 6, W6_AXIS, W6_DIAG), row.astype(F32)]
        for k, term in enumerate(terms):
            term_ref[bx, k : k + 1, :] = term
        kept = (iota((256, links), 0) == slot).astype(F32).astype(BF16)
        arrived = (iota((LANE, links), 0) + 256 == slot).astype(F32).astype(BF16)
        arrived_ref[bx] = arrived
        picked = dot_nn(kept_parts, kept) + dot_nn(stay_parts, arrived)
        pick_ref[bx] = picked[0:16] + picked[16:32] + picked[32:48]
        spread = (iota((LANE, links), 0) == side * 64 + cell % 64).astype(F32).astype(BF16)
        spread_ref[bx] = spread
        left = jnp.where(iota((8, links), 0) == row, direction.astype(F32), 0.0).astype(BF16)
        toward.append(dot_nt(left, spread))
    return jnp.concatenate(toward, axis=0)


def block_order(scratch_ref, plane):
    low_half = iota((8, LANE), 1) < 64
    scratch_ref[...] = plane
    even = scratch_ref[pl.ds(0, 8, stride=2), :]
    odd = scratch_ref[pl.ds(1, 8, stride=2), :]
    first = jnp.where(low_half, even, pltpu.roll(odd, 64, 1))
    second = jnp.where(low_half, pltpu.roll(even, 64, 1), odd)
    return first, second


def prepare_kernel(
    place_x_ref, place_y_ref, link_ref, col_ref, near_ref, far_ref, mine_ref, grains_ref, moves_ref, after_ref,
    plane_ref, value_ref, toward_ref, pick_ref, own_ref, arrived_ref, spread_ref, term_ref, scratch_ref,
):
    del after_ref
    lane = iota((ROWS, LANE), 1)
    kept = jnp.where(moves_ref[...] == 4, grains_ref[:, 0, :], 0.0)
    own_ref[...] = kept
    stay = jnp.where(one_of(iota((16, LANE), 1) // 8, (3, 4)), mine_ref[8:24, :], 0.0)
    kept_parts = jnp.concatenate(split3(kept[0:16]), axis=0)
    stay_parts = jnp.concatenate(split3(stay), axis=0)
    toward = link_maps(
        place_x_ref, place_y_ref, link_ref, kept_parts, stay_parts, arrived_ref, spread_ref, term_ref, pick_ref
    )
    for half, part in enumerate(block_order(scratch_ref.at[0], toward)):
        toward_ref[half] = part.astype(I32)
    ylo, yhi = from_pairs(place_y_ref, near_ref, far_ref, 0, ROWS)
    for q in range(Q):
        plane = y_shifted(q, col_ref[q], ylo, yhi, lane)
        if CX[q]:
            plane = pltpu.roll(plane, CX[q] % ROWS, 0)
        for ref, given in ((plane_ref, plane), (value_ref, col_ref[OPP[q]])):
            for half, part in enumerate(block_order(scratch_ref.at[q % 4 + (4 if ref is value_ref else 0)], given)):
                ref[q, half] = part


def table_kernel(mine_ref, xlo_ref, xhi_ref, own_ref, table_ref):
    grain_lane = iota((32, LANE), 1) // 8
    arrived = jnp.where(
        one_of(grain_lane, (5, 6, 7)),
        xlo_ref[8:, :],
        jnp.where(one_of(grain_lane, (0, 1, 2)), xhi_ref[8:, :], mine_ref[8:, :]),
    )
    table_ref[:, 0, 0:256] = own_ref[...]
    table_ref[:, 0, 256:320] = arrived[0:GV, 0:64]


def finish_kernel(
    owner_ref, plane_ref, value_ref, toward_ref, xlo_ref, xhi_ref, pick_ref,
    arrived_ref, spread_ref, term_ref, send_ref, scratch_ref,
):
    send_ref[...] = jnp.zeros(send_ref.shape, F32)
    grain_lane = iota((16, LANE), 1) // 8
    moved = jnp.where(
        one_of(grain_lane, (5, 6, 7)),
        xlo_ref[8:24, :],
        jnp.where(one_of(grain_lane, (0, 1, 2)), xhi_ref[8:24, :], 0.0),
    )
    moved_parts = jnp.concatenate(split3(moved), axis=0)
    corrections = []
    for bx in range(2):
        picked = dot_nn(moved_parts, arrived_ref[bx])
        g = pick_ref[bx] + (picked[0:16] + picked[16:32] + picked[32:48])
        mid_x, mid_y, mid_z, step_x, step_y, step_z, scale, at = (term_ref[bx, k : k + 1, :] for k in range(8))
        rel_x = mid_x - g[0:1]
        rel_y = mid_y - g[1:2]
        rel_z = mid_z - g[2:3]
        wall_x = g[3:4] + g[7:8] * rel_z - g[8:9] * rel_y
        wall_y = g[4:5] + g[8:9] * rel_x - g[6:7] * rel_z
        wall_z = g[5:6] + g[6:7] * rel_y - g[7:8] * rel_x
        correction = scale * (step_x * wall_x + step_y * wall_y + step_z * wall_z)
        here = iota((8, correction.shape[1]), 0) == at.astype(I32)
        left = jnp.concatenate(
            [jnp.where(here, part.astype(F32), 0.0) for part in split3(correction)], axis=0
        ).astype(BF16)
        dense = dot_nt(left, spread_ref[bx])
        corrections.append(dense[0:8] + dense[8:16] + dense[16:24])
    correction = jnp.concatenate(corrections, axis=0)
    correction = block_order(scratch_ref, correction)
    base = [owner_ref[n // 2, n % 2] * Q for n in range(4)]
    low_half = iota((8, LANE), 1) < 64
    row = iota((8, LANE), 0)
    first_row = jnp.logical_and(row == 0, low_half)
    last_row = jnp.logical_and(row == 7, jnp.logical_not(low_half))
    turned_low = pltpu.roll(xlo_ref[0:8, :], 64, 1)
    turned_high = pltpu.roll(xhi_ref[0:8, :], 64, 1)
    for q in range(Q):
        for half in range(2):
            part = plane_ref[q, half]
            if CX[q] == 1:
                k = XUP.index(q)
                edge = turned_low[k : k + 1] if half else xlo_ref[k : k + 1, :]
                part = jnp.where(first_row, edge, part)
            elif CX[q] == -1:
                k = XDN.index(q)
                edge = xhi_ref[k : k + 1, :] if half else turned_high[k : k + 1]
                part = jnp.where(last_row, edge, part)
            if q:
                part = jnp.where(toward_ref[half] == OPP[q], value_ref[q, half] - correction[half], part)
            send_ref[base[half] + q] = part[0:4]
            send_ref[base[2 + half] + q] = part[4:8]


VMEM = pl.BlockSpec(memory_space=pltpu.VMEM)
SMEM = pl.BlockSpec(memory_space=pltpu.SMEM)


def ring(axis, step):
    count = lax.axis_size(axis)
    return [(i, (i + step) % count) for i in range(count)]


def pair_gather(message, axis, first):
    count = lax.axis_size(axis)
    groups = [[i, (i + 1) % count] for i in range(first, count, 2)]
    return lax.all_gather(message, axis, axis=0, tiled=True, axis_index_groups=groups)


def near(*arrays):
    return tuple(pltpu.with_memory_space_constraint(a, pltpu.VMEM) for a in arrays)


def chip(*dims, dtype=F32):
    return pltpu.VMEM(dims, dtype)


def body(pdf, grains, grain_moves, owner_map, link_lists):
    group = lax.axis_size("gx")
    place_x = lax.axis_index("gx").astype(I32).reshape(1)
    place_y = lax.axis_index("gy").astype(I32).reshape(1)
    links = link_lists.shape[2]
    col, near_msg, far_msg = pl.pallas_call(
        first_kernel,
        out_shape=(chip(Q, ROWS, LANE), chip(48, LANE), chip(48, LANE)),
        in_specs=[SMEM] + [VMEM] * 3,
        out_specs=(VMEM,) * 3,
        name="collide_pack",
    )(place_y, pdf, grains, grain_moves)
    near_pair = pair_gather(near_msg, "gy", 0)
    near_pair, far_msg = lax.optimization_barrier((near_pair, far_msg))
    far_pair = pair_gather(far_msg, "gy", 1)
    x_up, x_dn = pl.pallas_call(
        second_kernel,
        out_shape=(chip(40, LANE), chip(40, LANE)),
        in_specs=[SMEM] + [VMEM] * 4,
        out_specs=(VMEM,) * 2,
        name="x_messages",
    )(place_y, *near(col, near_msg, near_pair, far_pair))
    xlo = lax.ppermute(x_up, "gx", ring("gx", 1))
    xhi = lax.ppermute(x_dn, "gx", ring("gx", -1))
    plane, value, toward, pick, own, arrived, spread, terms = pl.pallas_call(
        prepare_kernel,
        out_shape=(
            chip(Q, 2, 8, LANE),
            chip(Q, 2, 8, LANE),
            chip(2, 8, LANE, dtype=I32),
            chip(2, 16, links),
            chip(GV, 256),
            chip(2, LANE, links, dtype=BF16),
            chip(2, LANE, links, dtype=BF16),
            chip(2, 8, links),
        ),
        in_specs=[SMEM, SMEM] + [VMEM] * 8,
        out_specs=(VMEM,) * 8,
        scratch_shapes=[pltpu.VMEM((8, ROWS, LANE), F32)],
        cost_estimate=pl.CostEstimate(flops=4_000_000, bytes_accessed=1_000_000, transcendentals=0),
        name="prepare",
    )(place_x, place_y, link_lists, *near(col, near_pair, far_pair, x_up), grains, grain_moves, *near(x_dn))
    send = pl.pallas_call(
        finish_kernel,
        out_shape=jax.ShapeDtypeStruct((group * Q, 4, LANE), F32),
        in_specs=[SMEM] + [VMEM] * 9,
        out_specs=VMEM,
        scratch_shapes=[pltpu.VMEM((ROWS, LANE), F32)],
        name="finish_blocks",
    )(owner_map, *near(plane, value, toward, xlo, xhi, pick, arrived, spread, terms))
    table = pl.pallas_call(
        table_kernel,
        out_shape=jax.ShapeDtypeStruct((GV, 1, 320), F32),
        in_specs=[VMEM] * 4,
        out_specs=VMEM,
        name="grain_table",
    )(*near(x_up, xlo, xhi, own))
    out = lax.all_to_all(send.reshape(group, 1, Q, 512), "gx", split_axis=0, concat_axis=0, tiled=True)
    return (out, table)


def solution(mesh):
    in_specs = (
        P(None, "gx", "gy"),
        P(None, "gx", "gy"),
        P("gx", "gy"),
        P("gx", "gy"),
        P(None, "gx", "gy"),
    )
    out_specs = (P("gx", "gy", None, None), P(None, "gx", "gy"))
    return jax.shard_map(body, mesh=mesh, in_specs=in_specs, out_specs=out_specs, check_vma=False)
```

```python
import jax
import jax.numpy as jnp
import numpy as np
from jax import lax
from jax.experimental import pallas as pl
from jax.experimental.pallas import tpu as pltpu
from jax.sharding import PartitionSpec as P

Q = 19
E = 8
Z = 8
ROWS = 16
LANE = 128
GV = 26

CX = (0, 1, -1, 0, 0, 0, 0, 1, -1, 1, -1, 1, -1, 1, -1, 0, 0, 0, 0)
CY = (0, 0, 0, 1, -1, 0, 0, 1, -1, -1, 1, 0, 0, 0, 0, 1, -1, 1, -1)
CZ = (0, 0, 0, 0, 0, 1, -1, 0, 0, 0, 0, 1, -1, -1, 1, 1, -1, -1, 1)
OPP = (0, 2, 1, 4, 3, 6, 5, 8, 7, 10, 9, 12, 11, 14, 13, 16, 15, 18, 17)
WTS = tuple(float(np.float32(w)) for w in [1.0 / 3.0] + [1.0 / 18.0] * 6 + [1.0 / 36.0] * 12)
W6_AXIS = float(np.float32(6.0) * np.float32(1.0 / 18.0))
W6_DIAG = float(np.float32(6.0) * np.float32(1.0 / 36.0))
XUP = tuple(q for q in range(Q) if CX[q] == 1)
XDN = tuple(q for q in range(Q) if CX[q] == -1)
YUP = tuple(q for q in range(Q) if CY[q] == 1)
YDN = tuple(q for q in range(Q) if CY[q] == -1)
CODES = (0, 1, 2, 3, 5, 6, 7, 8)

F32 = jnp.float32
BF16 = jnp.bfloat16
I32 = jnp.int32


def iota(shape, dim):
    return lax.broadcasted_iota(I32, shape, dim)


def split3(value):
    high = value.astype(BF16)
    rest = value - high.astype(F32)
    middle = rest.astype(BF16)
    low = (rest - middle.astype(F32)).astype(BF16)
    return high, middle, low


def dot_nt(a, b):
    return lax.dot_general(a, b, (((1,), (1,)), ((), ())), preferred_element_type=F32)


def dot_nn(a, b):
    return lax.dot_general(a, b, (((1,), (0,)), ((), ())), preferred_element_type=F32)


def one_of(index, chosen):
    hit = index == chosen[0]
    for value in chosen[1:]:
        hit = jnp.logical_or(hit, index == value)
    return hit


def z_shift(plane, step, lane):
    depth = lane % Z
    if step == 1:
        return jnp.where(depth == 0, pltpu.roll(plane, LANE - (Z - 1), 1), pltpu.roll(plane, 1, 1))
    if step == -1:
        return jnp.where(depth == Z - 1, pltpu.roll(plane, Z - 1, 1), pltpu.roll(plane, LANE - 1, 1))
    return plane


def collide(f):
    s = {q: f[q] + f[q + 1] for q in range(1, Q, 2)}
    d = {q: f[q] - f[q + 1] for q in range(1, Q, 2)}
    pxx = s[1] + s[7] + s[9] + s[11] + s[13]
    pyy = s[3] + s[7] + s[9] + s[15] + s[17]
    pzz = s[5] + s[11] + s[13] + s[15] + s[17]
    pxy = s[7] - s[9]
    pxz = s[11] - s[13]
    pyz = s[15] - s[17]
    rho = f[0] + s[1] + s[3] + s[5] + s[7] + s[9] + s[11] + s[13] + s[15] + s[17]
    inv_rho = 1.0 / rho
    ux = (d[1] + d[7] + d[9] + d[11] + d[13]) * inv_rho
    uy = (d[3] + d[7] - d[9] + d[15] + d[17]) * inv_rho
    uz = (d[5] + d[11] - d[13] + d[15] - d[17]) * inv_rho
    third = rho * (1.0 / 3.0)
    sxx = pxx - third - rho * ux * ux
    syy = pyy - third - rho * uy * uy
    szz = pzz - third - rho * uz * uz
    sxy = pxy - rho * ux * uy
    sxz = pxz - rho * ux * uz
    syz = pyz - rho * uy * uz
    contracted = sxx * sxx + syy * syy + szz * szz + 2.0 * (sxy * sxy + sxz * sxz + syz * syz)
    rate = 1.5 / 0.8 * inv_rho * jnp.sqrt(2.0 * contracted)
    scaled = 20.0 * rate
    viscosity = 0.01 + 0.09 * lax.rsqrt(jnp.sqrt(1.0 + scaled * scaled))
    omega = 1.0 / (3.0 * viscosity + 0.5)
    speed = 1.0 - 1.5 * (ux * ux + uy * uy + uz * uz)
    vel = (ux, uy, uz)
    out = [None] * Q
    out[0] = f[0] - (f[0] - WTS[0] * rho * speed) * omega
    for q in range(1, Q, 2):
        proj = None
        for comp, step in zip(vel, (CX[q], CY[q], CZ[q])):
            if step:
                term = comp if step > 0 else -comp
                proj = term if proj is None else proj + term
        scale = WTS[q] * rho
        even = scale * (speed + 4.5 * proj * proj)
        odd = scale * (3.0 * proj)
        out[q] = f[q] - (f[q] - (even + odd)) * omega
        out[q + 1] = f[q + 1] - (f[q + 1] - (even - odd)) * omega
    return out


def first_kernel(place_y_ref, pdf_ref, grains_ref, moves_ref, col_ref, near_ref, far_ref):
    lane = iota((ROWS, LANE), 1)
    col = collide([pdf_ref[q] for q in range(Q)])
    for q in range(Q):
        col_ref[q] = col[q]
    rims = []
    for chosen, edge in ((YUP, LANE - Z), (YDN, 0)):
        rim = jnp.zeros((ROWS, LANE), F32)
        for k, q in enumerate(chosen):
            moved = pltpu.roll(z_shift(col[q], CZ[q], lane), (k * Z - edge) % LANE, 1)
            rim = jnp.where(lane // Z == k, moved, rim)
        rims.append(rim)
    left = place_y_ref[0] % 2 == 0
    near_ref[0:ROWS, :] = jnp.where(left, rims[0], rims[1])
    far_ref[0:ROWS, :] = jnp.where(left, rims[1], rims[0])
    moves = moves_ref[...]
    count = moves.shape[1]
    matches = (iota((16, count), 0) == moves).astype(F32)
    earlier = (iota((count, count), 0) < iota((count, count), 1)).astype(F32).astype(BF16)
    before = dot_nn(matches.astype(BF16), earlier)
    rank = jnp.sum(matches * before, axis=0, keepdims=True).astype(I32)
    region = jnp.where(moves > 4, moves - 1, moves)
    target = jnp.where(moves == 4, -1, region * 8 + rank)
    placing = (iota((LANE, count), 0) == target).astype(F32).astype(BF16)
    own = grains_ref[:, 0, :]
    high, middle, low = split3(own)
    packed = dot_nt(high, placing) + dot_nt(middle, placing) + dot_nt(low, placing)
    for ref in (near_ref, far_ref):
        ref[ROWS : ROWS + GV, :] = packed
        ref[ROWS + GV :, :] = jnp.zeros((6, LANE), F32)


def y_shifted(q, plane, ylo, yhi, lane):
    plane = z_shift(plane, CZ[q], lane)
    if CY[q] == 1:
        k = YUP.index(q)
        return jnp.where(lane < Z, pltpu.roll(ylo, (LANE - k * Z) % LANE, 1), pltpu.roll(plane, Z, 1))
    if CY[q] == -1:
        k = YDN.index(q)
        return jnp.where(
            lane >= LANE - Z,
            pltpu.roll(yhi, (LANE - Z - k * Z) % LANE, 1),
            pltpu.roll(plane, LANE - Z, 1),
        )
    return plane


def from_pairs(place_y_ref, near_ref, far_ref, start, size):
    left = place_y_ref[0] % 2 == 0
    low = slice(start, start + size)
    high = slice(48 + start, 48 + start + size)
    far = far_ref[low, :]
    ylo = jnp.where(left, far, near_ref[low, :])
    yhi = jnp.where(left, near_ref[high, :], far)
    return ylo, yhi


def second_kernel(place_y_ref, col_ref, mine_ref, near_ref, far_ref, up_ref, dn_ref):
    lane = iota((8, LANE), 1)
    for ref, chosen, part, row in ((up_ref, XUP, 8, 7), (dn_ref, XDN, 0, 0)):
        ref[0:8, :] = jnp.zeros((8, LANE), F32)
        ylo, yhi = from_pairs(place_y_ref, near_ref, far_ref, part, 8)
        for k, q in enumerate(chosen):
            shifted = y_shifted(q, col_ref[q, part : part + 8, :], ylo, yhi, lane)
            ref[k : k + 1, :] = shifted[row : row + 1, :]
    grain_lane = iota((32, LANE), 1) // 8
    ylo, yhi = from_pairs(place_y_ref, near_ref, far_ref, ROWS, 32)
    joined = jnp.where(
        one_of(grain_lane, (2, 4, 7)), ylo, jnp.where(one_of(grain_lane, (0, 3, 5)), yhi, mine_ref[ROWS:, :])
    )
    up_ref[8:, :] = joined
    dn_ref[8:, :] = joined


def link_maps(place_x_ref, place_y_ref, link_ref, kept_parts, stay_parts, arrived_ref, spread_ref, term_ref, pick_ref):
    toward = []
    for bx in range(2):
        cell = link_ref[0, bx : bx + 1, :]
        direction = link_ref[1, bx : bx + 1, :]
        slot = link_ref[2, bx : bx + 1, :]
        links = cell.shape[1]
        side = iota((1, links), 1) // 256

        def component(table):
            plus = one_of(direction, [q for q in range(Q) if table[q] == 1])
            minus = one_of(direction, [q for q in range(Q) if table[q] == -1])
            return jnp.where(plus, 1.0, jnp.where(minus, -1.0, 0.0))

        steps = [component(table) for table in (CX, CY, CZ)]
        corner = (
            (place_x_ref[0] * 2 + bx) * E + cell // (E * Z),
            (place_y_ref[0] * 2 + side) * E + cell // Z % E,
            cell % Z,
        )
        row = cell // (E * Z)
        terms = [c.astype(F32) + 0.5 * step for c, step in zip(corner, steps)] + steps
        terms += [jnp.where(direction <= 6, W6_AXIS, W6_DIAG), row.astype(F32)]
        for k, term in enumerate(terms):
            term_ref[bx, k : k + 1, :] = term
        kept = (iota((256, links), 0) == slot).astype(F32).astype(BF16)
        arrived = (iota((LANE, links), 0) + 256 == slot).astype(F32).astype(BF16)
        arrived_ref[bx] = arrived
        picked = dot_nn(kept_parts, kept) + dot_nn(stay_parts, arrived)
        pick_ref[bx] = picked[0:16] + picked[16:32] + picked[32:48]
        spread = (iota((LANE, links), 0) == side * 64 + cell % 64).astype(F32).astype(BF16)
        spread_ref[bx] = spread
        left = jnp.where(iota((8, links), 0) == row, direction.astype(F32), 0.0).astype(BF16)
        toward.append(dot_nt(left, spread))
    return jnp.concatenate(toward, axis=0)


def block_order(scratch_ref, plane):
    low_half = iota((8, LANE), 1) < 64
    scratch_ref[...] = plane
    even = scratch_ref[pl.ds(0, 8, stride=2), :]
    odd = scratch_ref[pl.ds(1, 8, stride=2), :]
    first = jnp.where(low_half, even, pltpu.roll(odd, 64, 1))
    second = jnp.where(low_half, pltpu.roll(even, 64, 1), odd)
    return first, second


def prepare_kernel(
    place_x_ref, place_y_ref, link_ref, col_ref, near_ref, far_ref, mine_ref, grains_ref, moves_ref, after_ref,
    plane_ref, value_ref, toward_ref, pick_ref, own_ref, arrived_ref, spread_ref, term_ref, scratch_ref,
):
    del after_ref
    lane = iota((ROWS, LANE), 1)
    kept = jnp.where(moves_ref[...] == 4, grains_ref[:, 0, :], 0.0)
    own_ref[...] = kept
    stay = jnp.where(one_of(iota((16, LANE), 1) // 8, (3, 4)), mine_ref[8:24, :], 0.0)
    kept_parts = jnp.concatenate(split3(kept[0:16]), axis=0)
    stay_parts = jnp.concatenate(split3(stay), axis=0)
    toward = link_maps(
        place_x_ref, place_y_ref, link_ref, kept_parts, stay_parts, arrived_ref, spread_ref, term_ref, pick_ref
    )
    for half, part in enumerate(block_order(scratch_ref.at[0], toward)):
        toward_ref[half] = part.astype(I32)
    ylo, yhi = from_pairs(place_y_ref, near_ref, far_ref, 0, ROWS)
    for q in range(Q):
        plane = y_shifted(q, col_ref[q], ylo, yhi, lane)
        if CX[q]:
            plane = pltpu.roll(plane, CX[q] % ROWS, 0)
        for ref, given in ((plane_ref, plane), (value_ref, col_ref[OPP[q]])):
            for half, part in enumerate(block_order(scratch_ref.at[q % 4 + (4 if ref is value_ref else 0)], given)):
                ref[q, half] = part


def table_kernel(mine_ref, xlo_ref, xhi_ref, own_ref, table_ref):
    grain_lane = iota((32, LANE), 1) // 8
    arrived = jnp.where(
        one_of(grain_lane, (5, 6, 7)),
        xlo_ref[8:, :],
        jnp.where(one_of(grain_lane, (0, 1, 2)), xhi_ref[8:, :], mine_ref[8:, :]),
    )
    table_ref[:, 0, 0:256] = own_ref[...]
    table_ref[:, 0, 256:320] = arrived[0:GV, 0:64]


def finish_kernel(
    owner_ref, empty_ref, plane_ref, value_ref, toward_ref, xlo_ref, xhi_ref, pick_ref,
    arrived_ref, spread_ref, term_ref, send_ref, scratch_ref, block_ref, sems,
):
    del empty_ref
    grain_lane = iota((16, LANE), 1) // 8
    moved = jnp.where(
        one_of(grain_lane, (5, 6, 7)),
        xlo_ref[8:24, :],
        jnp.where(one_of(grain_lane, (0, 1, 2)), xhi_ref[8:24, :], 0.0),
    )
    moved_parts = jnp.concatenate(split3(moved), axis=0)
    corrections = []
    for bx in range(2):
        picked = dot_nn(moved_parts, arrived_ref[bx])
        g = pick_ref[bx] + (picked[0:16] + picked[16:32] + picked[32:48])
        mid_x, mid_y, mid_z, step_x, step_y, step_z, scale, at = (term_ref[bx, k : k + 1, :] for k in range(8))
        rel_x = mid_x - g[0:1]
        rel_y = mid_y - g[1:2]
        rel_z = mid_z - g[2:3]
        wall_x = g[3:4] + g[7:8] * rel_z - g[8:9] * rel_y
        wall_y = g[4:5] + g[8:9] * rel_x - g[6:7] * rel_z
        wall_z = g[5:6] + g[6:7] * rel_y - g[7:8] * rel_x
        correction = scale * (step_x * wall_x + step_y * wall_y + step_z * wall_z)
        here = iota((8, correction.shape[1]), 0) == at.astype(I32)
        left = jnp.concatenate(
            [jnp.where(here, part.astype(F32), 0.0) for part in split3(correction)], axis=0
        ).astype(BF16)
        dense = dot_nt(left, spread_ref[bx])
        corrections.append(dense[0:8] + dense[8:16] + dense[16:24])
    correction = jnp.concatenate(corrections, axis=0)
    correction = block_order(scratch_ref, correction)
    low_half = iota((8, LANE), 1) < 64
    row = iota((8, LANE), 0)
    first_row = jnp.logical_and(row == 0, low_half)
    last_row = jnp.logical_and(row == 7, jnp.logical_not(low_half))
    turned_low = pltpu.roll(xlo_ref[0:8, :], 64, 1)
    turned_high = pltpu.roll(xhi_ref[0:8, :], 64, 1)
    for q in range(Q):
        for half in range(2):
            part = plane_ref[q, half]
            if CX[q] == 1:
                k = XUP.index(q)
                edge = turned_low[k : k + 1] if half else xlo_ref[k : k + 1, :]
                part = jnp.where(first_row, edge, part)
            elif CX[q] == -1:
                k = XDN.index(q)
                edge = xhi_ref[k : k + 1, :] if half else turned_high[k : k + 1]
                part = jnp.where(last_row, edge, part)
            if q:
                part = jnp.where(toward_ref[half] == OPP[q], value_ref[q, half] - correction[half], part)
            block_ref[half, q] = part[0:4]
            block_ref[2 + half, q] = part[4:8]
    stores = [
        pltpu.make_async_copy(block_ref.at[n], send_ref.at[pl.ds(owner_ref[n // 2, n % 2] * Q, Q)], sems.at[n])
        for n in range(4)
    ]
    for copy in stores:
        copy.start()
    for copy in stores:
        copy.wait()


def clear_kernel(after_ref, send_ref):
    del after_ref
    send_ref[...] = jnp.zeros(send_ref.shape, F32)


VMEM = pl.BlockSpec(memory_space=pltpu.VMEM)
SMEM = pl.BlockSpec(memory_space=pltpu.SMEM)


def ring(axis, step):
    count = lax.axis_size(axis)
    return [(i, (i + step) % count) for i in range(count)]


def near(*arrays):
    return tuple(pltpu.with_memory_space_constraint(a, pltpu.VMEM) for a in arrays)


def chip(*dims, dtype=F32):
    return pltpu.VMEM(dims, dtype)


def body(pdf, grains, grain_moves, owner_map, link_lists):
    group = lax.axis_size("gx")
    place_x = lax.axis_index("gx").astype(I32).reshape(1)
    place_y = lax.axis_index("gy").astype(I32).reshape(1)
    links = link_lists.shape[2]
    col, near_msg, far_msg = pl.pallas_call(
        first_kernel,
        out_shape=(chip(Q, ROWS, LANE), chip(48, LANE), chip(48, LANE)),
        in_specs=[SMEM] + [VMEM] * 3,
        out_specs=(VMEM,) * 3,
        name="collide_pack",
    )(place_y, pdf, grains, grain_moves)
    columns = lax.axis_size("gy")
    far_pair = lax.ppermute(far_msg, "gy", [(i, (i + 2 * (i % 2) - 1) % columns) for i in range(columns)])
    near_pair = lax.all_gather(
        near_msg, "gy", axis=0, tiled=True, axis_index_groups=[[i, i + 1] for i in range(0, columns, 2)]
    )
    x_up, x_dn = pl.pallas_call(
        second_kernel,
        out_shape=(chip(40, LANE), chip(40, LANE)),
        in_specs=[SMEM] + [VMEM] * 4,
        out_specs=(VMEM,) * 2,
        name="x_messages",
    )(place_y, *near(col, near_msg, near_pair, far_pair))
    xlo = lax.ppermute(x_up, "gx", ring("gx", 1))
    xhi = lax.ppermute(x_dn, "gx", ring("gx", -1))
    plane, value, toward, pick, own, arrived, spread, terms = pl.pallas_call(
        prepare_kernel,
        out_shape=(
            chip(Q, 2, 8, LANE),
            chip(Q, 2, 8, LANE),
            chip(2, 8, LANE, dtype=I32),
            chip(2, 16, links),
            chip(GV, 256),
            chip(2, LANE, links, dtype=BF16),
            chip(2, LANE, links, dtype=BF16),
            chip(2, 8, links),
        ),
        in_specs=[SMEM, SMEM] + [VMEM] * 8,
        out_specs=(VMEM,) * 8,
        scratch_shapes=[pltpu.VMEM((8, ROWS, LANE), F32)],
        cost_estimate=pl.CostEstimate(flops=4_000_000, bytes_accessed=1_000_000, transcendentals=0),
        name="prepare",
    )(place_x, place_y, link_lists, *near(col, near_pair, far_pair, x_up), grains, grain_moves, *near(x_dn))
    empty = pl.pallas_call(
        clear_kernel,
        out_shape=jax.ShapeDtypeStruct((group * Q, 4, LANE), F32),
        in_specs=[VMEM],
        out_specs=VMEM,
        cost_estimate=pl.CostEstimate(flops=4_000_000, bytes_accessed=1_000_000, transcendentals=0),
        name="clear_slots",
    )(*near(x_dn))
    send = pl.pallas_call(
        finish_kernel,
        out_shape=jax.ShapeDtypeStruct((group * Q, 4, LANE), F32),
        in_specs=[SMEM, pl.BlockSpec(memory_space=pl.ANY)] + [VMEM] * 9,
        out_specs=pl.BlockSpec(memory_space=pl.ANY),
        input_output_aliases={1: 0},
        scratch_shapes=[
            pltpu.VMEM((ROWS, LANE), F32),
            pltpu.VMEM((4, Q, 4, LANE), F32),
            pltpu.SemaphoreType.DMA((4,)),
        ],
        name="finish_blocks",
    )(owner_map, empty, *near(plane, value, toward, xlo, xhi, pick, arrived, spread, terms))
    table = pl.pallas_call(
        table_kernel,
        out_shape=jax.ShapeDtypeStruct((GV, 1, 320), F32),
        in_specs=[VMEM] * 4,
        out_specs=VMEM,
        name="grain_table",
    )(*near(x_up, xlo, xhi, own))
    out = lax.all_to_all(send.reshape(group, 1, Q, 512), "gx", split_axis=0, concat_axis=0, tiled=True)
    return (out, table)


def solution(mesh):
    in_specs = (
        P(None, "gx", "gy"),
        P(None, "gx", "gy"),
        P("gx", "gy"),
        P("gx", "gy"),
        P(None, "gx", "gy"),
    )
    out_specs = (P("gx", "gy", None, None), P(None, "gx", "gy"))
    return jax.shard_map(body, mesh=mesh, in_specs=in_specs, out_specs=out_specs, check_vma=False)
```

```python
import jax
import jax.numpy as jnp
import numpy as np
from jax import lax
from jax.experimental import pallas as pl
from jax.experimental.pallas import tpu as pltpu
from jax.sharding import PartitionSpec as P

Q = 19
E = 8
Z = 8
ROWS = 16
LANE = 128
GV = 26

CX = (0, 1, -1, 0, 0, 0, 0, 1, -1, 1, -1, 1, -1, 1, -1, 0, 0, 0, 0)
CY = (0, 0, 0, 1, -1, 0, 0, 1, -1, -1, 1, 0, 0, 0, 0, 1, -1, 1, -1)
CZ = (0, 0, 0, 0, 0, 1, -1, 0, 0, 0, 0, 1, -1, -1, 1, 1, -1, -1, 1)
OPP = (0, 2, 1, 4, 3, 6, 5, 8, 7, 10, 9, 12, 11, 14, 13, 16, 15, 18, 17)
WTS = tuple(float(np.float32(w)) for w in [1.0 / 3.0] + [1.0 / 18.0] * 6 + [1.0 / 36.0] * 12)
W6_AXIS = float(np.float32(6.0) * np.float32(1.0 / 18.0))
W6_DIAG = float(np.float32(6.0) * np.float32(1.0 / 36.0))
XUP = tuple(q for q in range(Q) if CX[q] == 1)
XDN = tuple(q for q in range(Q) if CX[q] == -1)
YUP = tuple(q for q in range(Q) if CY[q] == 1)
YDN = tuple(q for q in range(Q) if CY[q] == -1)
CODES = (0, 1, 2, 3, 5, 6, 7, 8)

F32 = jnp.float32
BF16 = jnp.bfloat16
I32 = jnp.int32


def iota(shape, dim):
    return lax.broadcasted_iota(I32, shape, dim)


def split3(value):
    high = value.astype(BF16)
    rest = value - high.astype(F32)
    middle = rest.astype(BF16)
    low = (rest - middle.astype(F32)).astype(BF16)
    return high, middle, low


def dot_nt(a, b):
    return lax.dot_general(a, b, (((1,), (1,)), ((), ())), preferred_element_type=F32)


def dot_nn(a, b):
    return lax.dot_general(a, b, (((1,), (0,)), ((), ())), preferred_element_type=F32)


def one_of(index, chosen):
    hit = index == chosen[0]
    for value in chosen[1:]:
        hit = jnp.logical_or(hit, index == value)
    return hit


def z_shift(plane, step, lane):
    depth = lane % Z
    if step == 1:
        return jnp.where(depth == 0, pltpu.roll(plane, LANE - (Z - 1), 1), pltpu.roll(plane, 1, 1))
    if step == -1:
        return jnp.where(depth == Z - 1, pltpu.roll(plane, Z - 1, 1), pltpu.roll(plane, LANE - 1, 1))
    return plane


def collide(f):
    s = {q: f[q] + f[q + 1] for q in range(1, Q, 2)}
    d = {q: f[q] - f[q + 1] for q in range(1, Q, 2)}
    pxx = s[1] + s[7] + s[9] + s[11] + s[13]
    pyy = s[3] + s[7] + s[9] + s[15] + s[17]
    pzz = s[5] + s[11] + s[13] + s[15] + s[17]
    pxy = s[7] - s[9]
    pxz = s[11] - s[13]
    pyz = s[15] - s[17]
    rho = f[0] + s[1] + s[3] + s[5] + s[7] + s[9] + s[11] + s[13] + s[15] + s[17]
    inv_rho = 1.0 / rho
    ux = (d[1] + d[7] + d[9] + d[11] + d[13]) * inv_rho
    uy = (d[3] + d[7] - d[9] + d[15] + d[17]) * inv_rho
    uz = (d[5] + d[11] - d[13] + d[15] - d[17]) * inv_rho
    third = rho * (1.0 / 3.0)
    sxx = pxx - third - rho * ux * ux
    syy = pyy - third - rho * uy * uy
    szz = pzz - third - rho * uz * uz
    sxy = pxy - rho * ux * uy
    sxz = pxz - rho * ux * uz
    syz = pyz - rho * uy * uz
    contracted = sxx * sxx + syy * syy + szz * szz + 2.0 * (sxy * sxy + sxz * sxz + syz * syz)
    rate = 1.5 / 0.8 * inv_rho * jnp.sqrt(2.0 * contracted)
    scaled = 20.0 * rate
    viscosity = 0.01 + 0.09 * lax.rsqrt(jnp.sqrt(1.0 + scaled * scaled))
    omega = 1.0 / (3.0 * viscosity + 0.5)
    speed = 1.0 - 1.5 * (ux * ux + uy * uy + uz * uz)
    vel = (ux, uy, uz)
    out = [None] * Q
    out[0] = f[0] - (f[0] - WTS[0] * rho * speed) * omega
    for q in range(1, Q, 2):
        proj = None
        for comp, step in zip(vel, (CX[q], CY[q], CZ[q])):
            if step:
                term = comp if step > 0 else -comp
                proj = term if proj is None else proj + term
        scale = WTS[q] * rho
        even = scale * (speed + 4.5 * proj * proj)
        odd = scale * (3.0 * proj)
        out[q] = f[q] - (f[q] - (even + odd)) * omega
        out[q + 1] = f[q + 1] - (f[q + 1] - (even - odd)) * omega
    return out


def first_kernel(place_y_ref, pdf_ref, grains_ref, moves_ref, col_ref, near_ref, far_ref):
    lane = iota((ROWS, LANE), 1)
    col = collide([pdf_ref[q] for q in range(Q)])
    for q in range(Q):
        col_ref[q] = col[q]
    rims = []
    for chosen, edge in ((YUP, LANE - Z), (YDN, 0)):
        rim = jnp.zeros((ROWS, LANE), F32)
        for k, q in enumerate(chosen):
            moved = pltpu.roll(z_shift(col[q], CZ[q], lane), (k * Z - edge) % LANE, 1)
            rim = jnp.where(lane // Z == k, moved, rim)
        rims.append(rim)
    left = place_y_ref[0] % 2 == 0
    near_ref[0:ROWS, :] = jnp.where(left, rims[0], rims[1])
    far_ref[0:ROWS, :] = jnp.where(left, rims[1], rims[0])
    moves = moves_ref[...]
    count = moves.shape[1]
    matches = (iota((16, count), 0) == moves).astype(F32)
    earlier = (iota((count, count), 0) < iota((count, count), 1)).astype(F32).astype(BF16)
    before = dot_nn(matches.astype(BF16), earlier)
    rank = jnp.sum(matches * before, axis=0, keepdims=True).astype(I32)
    region = jnp.where(moves > 4, moves - 1, moves)
    target = jnp.where(moves == 4, -1, region * 8 + rank)
    placing = (iota((LANE, count), 0) == target).astype(F32).astype(BF16)
    own = grains_ref[:, 0, :]
    high, middle, low = split3(own)
    packed = dot_nt(high, placing) + dot_nt(middle, placing) + dot_nt(low, placing)
    for ref in (near_ref, far_ref):
        ref[ROWS : ROWS + GV, :] = packed
        ref[ROWS + GV :, :] = jnp.zeros((6, LANE), F32)


def y_shifted(q, plane, ylo, yhi, lane):
    plane = z_shift(plane, CZ[q], lane)
    if CY[q] == 1:
        k = YUP.index(q)
        return jnp.where(lane < Z, pltpu.roll(ylo, (LANE - k * Z) % LANE, 1), pltpu.roll(plane, Z, 1))
    if CY[q] == -1:
        k = YDN.index(q)
        return jnp.where(
            lane >= LANE - Z,
            pltpu.roll(yhi, (LANE - Z - k * Z) % LANE, 1),
            pltpu.roll(plane, LANE - Z, 1),
        )
    return plane


def from_pairs(place_y_ref, near_ref, far_ref, start, size):
    left = place_y_ref[0] % 2 == 0
    low = slice(start, start + size)
    high = slice(48 + start, 48 + start + size)
    far = far_ref[low, :]
    ylo = jnp.where(left, far, near_ref[low, :])
    yhi = jnp.where(left, near_ref[high, :], far)
    return ylo, yhi


def second_kernel(place_x_ref, place_y_ref, col_ref, mine_ref, near_ref, far_ref, first_ref, other_ref):
    even = place_x_ref[0] % 2 == 0
    lane = iota((8, LANE), 1)
    rims = []
    for chosen, part, row in ((XUP, 8, 7), (XDN, 0, 0)):
        ylo, yhi = from_pairs(place_y_ref, near_ref, far_ref, part, 8)
        lines = []
        for q in chosen:
            shifted = y_shifted(q, col_ref[q, part : part + 8, :], ylo, yhi, lane)
            lines.append(shifted[row : row + 1, :])
        rims.append(jnp.concatenate(lines + [jnp.zeros((3, LANE), F32)], axis=0))
    first_ref[0:8, :] = jnp.where(even, rims[0], rims[1])
    other_ref[0:8, :] = jnp.where(even, rims[1], rims[0])
    grain_lane = iota((32, LANE), 1) // 8
    ylo, yhi = from_pairs(place_y_ref, near_ref, far_ref, ROWS, 32)
    joined = jnp.where(
        one_of(grain_lane, (2, 4, 7)), ylo, jnp.where(one_of(grain_lane, (0, 3, 5)), yhi, mine_ref[ROWS:, :])
    )
    first_ref[8:, :] = joined
    other_ref[8:, :] = joined


def from_rows(place_x_ref, first_ref, other_ref, start, size):
    even = place_x_ref[0] % 2 == 0
    first = first_ref[start : start + size, :]
    other = other_ref[start : start + size, :]
    return jnp.where(even, other, first), jnp.where(even, first, other)


def link_maps(place_x_ref, place_y_ref, link_ref, kept_parts, stay_parts, arrived_ref, spread_ref, term_ref, pick_ref):
    toward = []
    for bx in range(2):
        cell = link_ref[0, bx : bx + 1, :]
        direction = link_ref[1, bx : bx + 1, :]
        slot = link_ref[2, bx : bx + 1, :]
        links = cell.shape[1]
        side = iota((1, links), 1) // 256

        def component(table):
            plus = one_of(direction, [q for q in range(Q) if table[q] == 1])
            minus = one_of(direction, [q for q in range(Q) if table[q] == -1])
            return jnp.where(plus, 1.0, jnp.where(minus, -1.0, 0.0))

        steps = [component(table) for table in (CX, CY, CZ)]
        corner = (
            (place_x_ref[0] * 2 + bx) * E + cell // (E * Z),
            (place_y_ref[0] * 2 + side) * E + cell // Z % E,
            cell % Z,
        )
        row = cell // (E * Z)
        terms = [c.astype(F32) + 0.5 * step for c, step in zip(corner, steps)] + steps
        terms += [jnp.where(direction <= 6, W6_AXIS, W6_DIAG), row.astype(F32)]
        for k, term in enumerate(terms):
            term_ref[bx, k : k + 1, :] = term
        kept = (iota((256, links), 0) == slot).astype(F32).astype(BF16)
        arrived = (iota((LANE, links), 0) + 256 == slot).astype(F32).astype(BF16)
        arrived_ref[bx] = arrived
        picked = dot_nn(kept_parts, kept) + dot_nn(stay_parts, arrived)
        pick_ref[bx] = picked[0:16] + picked[16:32] + picked[32:48]
        spread = (iota((LANE, links), 0) == side * 64 + cell % 64).astype(F32).astype(BF16)
        spread_ref[bx] = spread
        left = jnp.where(iota((8, links), 0) == row, direction.astype(F32), 0.0).astype(BF16)
        toward.append(dot_nt(left, spread))
    return jnp.concatenate(toward, axis=0)


def block_order(scratch_ref, plane):
    low_half = iota((8, LANE), 1) < 64
    scratch_ref[...] = plane
    even = scratch_ref[pl.ds(0, 8, stride=2), :]
    odd = scratch_ref[pl.ds(1, 8, stride=2), :]
    first = jnp.where(low_half, even, pltpu.roll(odd, 64, 1))
    second = jnp.where(low_half, pltpu.roll(even, 64, 1), odd)
    return first, second


def prepare_kernel(
    place_x_ref, place_y_ref, link_ref, col_ref, near_ref, far_ref, mine_ref, grains_ref, moves_ref, after_ref,
    plane_ref, value_ref, toward_ref, pick_ref, own_ref, arrived_ref, spread_ref, term_ref, scratch_ref,
):
    del after_ref
    lane = iota((ROWS, LANE), 1)
    kept = jnp.where(moves_ref[...] == 4, grains_ref[:, 0, :], 0.0)
    own_ref[...] = kept
    stay = jnp.where(one_of(iota((16, LANE), 1) // 8, (3, 4)), mine_ref[8:24, :], 0.0)
    kept_parts = jnp.concatenate(split3(kept[0:16]), axis=0)
    stay_parts = jnp.concatenate(split3(stay), axis=0)
    toward = link_maps(
        place_x_ref, place_y_ref, link_ref, kept_parts, stay_parts, arrived_ref, spread_ref, term_ref, pick_ref
    )
    for half, part in enumerate(block_order(scratch_ref.at[0], toward)):
        toward_ref[half] = part.astype(I32)
    ylo, yhi = from_pairs(place_y_ref, near_ref, far_ref, 0, ROWS)
    for q in range(Q):
        plane = y_shifted(q, col_ref[q], ylo, yhi, lane)
        if CX[q]:
            plane = pltpu.roll(plane, CX[q] % ROWS, 0)
        for ref, given in ((plane_ref, plane), (value_ref, col_ref[OPP[q]])):
            for half, part in enumerate(block_order(scratch_ref.at[q % 4 + (4 if ref is value_ref else 0)], given)):
                ref[q, half] = part


def table_kernel(place_x_ref, mine_ref, first_ref, other_ref, own_ref, table_ref):
    xlo, xhi = from_rows(place_x_ref, first_ref, other_ref, 8, 32)
    grain_lane = iota((32, LANE), 1) // 8
    arrived = jnp.where(
        one_of(grain_lane, (5, 6, 7)),
        xlo,
        jnp.where(one_of(grain_lane, (0, 1, 2)), xhi, mine_ref[8:, :]),
    )
    table_ref[:, 0, 0:256] = own_ref[...]
    table_ref[:, 0, 256:320] = arrived[0:GV, 0:64]


def finish_kernel(
    owner_ref, place_x_ref, empty_ref, plane_ref, value_ref, toward_ref, first_ref, other_ref, pick_ref,
    arrived_ref, spread_ref, term_ref, send_ref, scratch_ref, block_ref, sems,
):
    del empty_ref
    grain_lane = iota((16, LANE), 1) // 8
    xlo, xhi = from_rows(place_x_ref, first_ref, other_ref, 8, 16)
    moved = jnp.where(one_of(grain_lane, (5, 6, 7)), xlo, jnp.where(one_of(grain_lane, (0, 1, 2)), xhi, 0.0))
    moved_parts = jnp.concatenate(split3(moved), axis=0)
    corrections = []
    for bx in range(2):
        picked = dot_nn(moved_parts, arrived_ref[bx])
        g = pick_ref[bx] + (picked[0:16] + picked[16:32] + picked[32:48])
        mid_x, mid_y, mid_z, step_x, step_y, step_z, scale, at = (term_ref[bx, k : k + 1, :] for k in range(8))
        rel_x = mid_x - g[0:1]
        rel_y = mid_y - g[1:2]
        rel_z = mid_z - g[2:3]
        wall_x = g[3:4] + g[7:8] * rel_z - g[8:9] * rel_y
        wall_y = g[4:5] + g[8:9] * rel_x - g[6:7] * rel_z
        wall_z = g[5:6] + g[6:7] * rel_y - g[7:8] * rel_x
        correction = scale * (step_x * wall_x + step_y * wall_y + step_z * wall_z)
        here = iota((8, correction.shape[1]), 0) == at.astype(I32)
        left = jnp.concatenate(
            [jnp.where(here, part.astype(F32), 0.0) for part in split3(correction)], axis=0
        ).astype(BF16)
        dense = dot_nt(left, spread_ref[bx])
        corrections.append(dense[0:8] + dense[8:16] + dense[16:24])
    correction = jnp.concatenate(corrections, axis=0)
    correction = block_order(scratch_ref, correction)
    low_half = iota((8, LANE), 1) < 64
    row = iota((8, LANE), 0)
    first_row = jnp.logical_and(row == 0, low_half)
    last_row = jnp.logical_and(row == 7, jnp.logical_not(low_half))
    rim_low, rim_high = from_rows(place_x_ref, first_ref, other_ref, 0, 8)
    turned_low = pltpu.roll(rim_low, 64, 1)
    turned_high = pltpu.roll(rim_high, 64, 1)
    for q in range(Q):
        for half in range(2):
            part = plane_ref[q, half]
            if CX[q] == 1:
                k = XUP.index(q)
                edge = turned_low[k : k + 1] if half else rim_low[k : k + 1]
                part = jnp.where(first_row, edge, part)
            elif CX[q] == -1:
                k = XDN.index(q)
                edge = rim_high[k : k + 1] if half else turned_high[k : k + 1]
                part = jnp.where(last_row, edge, part)
            if q:
                part = jnp.where(toward_ref[half] == OPP[q], value_ref[q, half] - correction[half], part)
            block_ref[half, q] = part[0:4]
            block_ref[2 + half, q] = part[4:8]
    stores = [
        pltpu.make_async_copy(block_ref.at[n], send_ref.at[pl.ds(owner_ref[n // 2, n % 2] * Q, Q)], sems.at[n])
        for n in range(4)
    ]
    for copy in stores:
        copy.start()
    for copy in stores:
        copy.wait()


def clear_kernel(after_ref, send_ref):
    del after_ref
    send_ref[...] = jnp.zeros(send_ref.shape, F32)


VMEM = pl.BlockSpec(memory_space=pltpu.VMEM)
SMEM = pl.BlockSpec(memory_space=pltpu.SMEM)


def near(*arrays):
    return tuple(pltpu.with_memory_space_constraint(a, pltpu.VMEM) for a in arrays)


def chip(*dims, dtype=F32):
    return pltpu.VMEM(dims, dtype)


def body(pdf, grains, grain_moves, owner_map, link_lists):
    group = lax.axis_size("gx")
    place_x = lax.axis_index("gx").astype(I32).reshape(1)
    place_y = lax.axis_index("gy").astype(I32).reshape(1)
    links = link_lists.shape[2]
    col, near_msg, far_msg = pl.pallas_call(
        first_kernel,
        out_shape=(chip(Q, ROWS, LANE), chip(48, LANE), chip(48, LANE)),
        in_specs=[SMEM] + [VMEM] * 3,
        out_specs=(VMEM,) * 3,
        name="collide_pack",
    )(place_y, pdf, grains, grain_moves)
    columns = lax.axis_size("gy")
    far_pair = lax.ppermute(far_msg, "gy", [(i, (i + 2 * (i % 2) - 1) % columns) for i in range(columns)])
    near_pair = lax.all_gather(
        near_msg, "gy", axis=0, tiled=True, axis_index_groups=[[i, i + 1] for i in range(0, columns, 2)]
    )
    x_first, x_other = pl.pallas_call(
        second_kernel,
        out_shape=(chip(40, LANE), chip(40, LANE)),
        in_specs=[SMEM] * 2 + [VMEM] * 4,
        out_specs=(VMEM,) * 2,
        name="x_messages",
    )(place_x, place_y, *near(col, near_msg, near_pair, far_pair))
    first = lax.ppermute(x_first, "gx", [(i, i ^ 1) for i in range(group)])
    other = lax.ppermute(x_other, "gx", [(i, (i + 2 * (i % 2) - 1) % group) for i in range(group)])
    plane, value, toward, pick, own, arrived, spread, terms = pl.pallas_call(
        prepare_kernel,
        out_shape=(
            chip(Q, 2, 8, LANE),
            chip(Q, 2, 8, LANE),
            chip(2, 8, LANE, dtype=I32),
            chip(2, 16, links),
            chip(GV, 256),
            chip(2, LANE, links, dtype=BF16),
            chip(2, LANE, links, dtype=BF16),
            chip(2, 8, links),
        ),
        in_specs=[SMEM, SMEM] + [VMEM] * 8,
        out_specs=(VMEM,) * 8,
        scratch_shapes=[pltpu.VMEM((8, ROWS, LANE), F32)],
        cost_estimate=pl.CostEstimate(flops=4_000_000, bytes_accessed=1_000_000, transcendentals=0),
        name="prepare",
    )(place_x, place_y, link_lists, *near(col, near_pair, far_pair, x_first), grains, grain_moves, *near(x_other))
    empty = pl.pallas_call(
        clear_kernel,
        out_shape=jax.ShapeDtypeStruct((group * Q, 4, LANE), F32),
        in_specs=[VMEM],
        out_specs=VMEM,
        cost_estimate=pl.CostEstimate(flops=4_000_000, bytes_accessed=1_000_000, transcendentals=0),
        name="clear_slots",
    )(*near(x_other))
    send = pl.pallas_call(
        finish_kernel,
        out_shape=jax.ShapeDtypeStruct((group * Q, 4, LANE), F32),
        in_specs=[SMEM, SMEM, pl.BlockSpec(memory_space=pl.ANY)] + [VMEM] * 9,
        out_specs=pl.BlockSpec(memory_space=pl.ANY),
        input_output_aliases={2: 0},
        scratch_shapes=[
            pltpu.VMEM((ROWS, LANE), F32),
            pltpu.VMEM((4, Q, 4, LANE), F32),
            pltpu.SemaphoreType.DMA((4,)),
        ],
        name="finish_blocks",
    )(owner_map, place_x, empty, *near(plane, value, toward, first, other, pick, arrived, spread, terms))
    table = pl.pallas_call(
        table_kernel,
        out_shape=jax.ShapeDtypeStruct((GV, 1, 320), F32),
        in_specs=[SMEM] + [VMEM] * 4,
        out_specs=VMEM,
        name="grain_table",
    )(place_x, *near(x_first, first, other, own))
    out = lax.all_to_all(send.reshape(group, 1, Q, 512), "gx", split_axis=0, concat_axis=0, tiled=True)
    return (out, table)


def solution(mesh):
    in_specs = (
        P(None, "gx", "gy"),
        P(None, "gx", "gy"),
        P("gx", "gy"),
        P("gx", "gy"),
        P(None, "gx", "gy"),
    )
    out_specs = (P("gx", "gy", None, None), P(None, "gx", "gy"))
    return jax.shard_map(body, mesh=mesh, in_specs=in_specs, out_specs=out_specs, check_vma=False)
```

```python
import jax
import jax.numpy as jnp
import numpy as np
from jax import lax
from jax.experimental import pallas as pl
from jax.experimental.pallas import tpu as pltpu
from jax.sharding import PartitionSpec as P

Q = 19
E = 8
Z = 8
ROWS = 16
LANE = 128
GV = 26

CX = (0, 1, -1, 0, 0, 0, 0, 1, -1, 1, -1, 1, -1, 1, -1, 0, 0, 0, 0)
CY = (0, 0, 0, 1, -1, 0, 0, 1, -1, -1, 1, 0, 0, 0, 0, 1, -1, 1, -1)
CZ = (0, 0, 0, 0, 0, 1, -1, 0, 0, 0, 0, 1, -1, -1, 1, 1, -1, -1, 1)
OPP = (0, 2, 1, 4, 3, 6, 5, 8, 7, 10, 9, 12, 11, 14, 13, 16, 15, 18, 17)
WTS = tuple(float(np.float32(w)) for w in [1.0 / 3.0] + [1.0 / 18.0] * 6 + [1.0 / 36.0] * 12)
W6_AXIS = float(np.float32(6.0) * np.float32(1.0 / 18.0))
W6_DIAG = float(np.float32(6.0) * np.float32(1.0 / 36.0))
XUP = tuple(q for q in range(Q) if CX[q] == 1)
XDN = tuple(q for q in range(Q) if CX[q] == -1)
YUP = tuple(q for q in range(Q) if CY[q] == 1)
YDN = tuple(q for q in range(Q) if CY[q] == -1)
CODES = (0, 1, 2, 3, 5, 6, 7, 8)

F32 = jnp.float32
BF16 = jnp.bfloat16
I32 = jnp.int32


def iota(shape, dim):
    return lax.broadcasted_iota(I32, shape, dim)


def split3(value):
    high = value.astype(BF16)
    rest = value - high.astype(F32)
    middle = rest.astype(BF16)
    low = (rest - middle.astype(F32)).astype(BF16)
    return high, middle, low


def dot_nt(a, b):
    return lax.dot_general(a, b, (((1,), (1,)), ((), ())), preferred_element_type=F32)


def dot_nn(a, b):
    return lax.dot_general(a, b, (((1,), (0,)), ((), ())), preferred_element_type=F32)


def one_of(index, chosen):
    hit = index == chosen[0]
    for value in chosen[1:]:
        hit = jnp.logical_or(hit, index == value)
    return hit


def z_shift(plane, step, lane):
    depth = lane % Z
    if step == 1:
        return jnp.where(depth == 0, pltpu.roll(plane, LANE - (Z - 1), 1), pltpu.roll(plane, 1, 1))
    if step == -1:
        return jnp.where(depth == Z - 1, pltpu.roll(plane, Z - 1, 1), pltpu.roll(plane, LANE - 1, 1))
    return plane


def collide(f):
    s = {q: f[q] + f[q + 1] for q in range(1, Q, 2)}
    d = {q: f[q] - f[q + 1] for q in range(1, Q, 2)}
    pxx = s[1] + s[7] + s[9] + s[11] + s[13]
    pyy = s[3] + s[7] + s[9] + s[15] + s[17]
    pzz = s[5] + s[11] + s[13] + s[15] + s[17]
    pxy = s[7] - s[9]
    pxz = s[11] - s[13]
    pyz = s[15] - s[17]
    rho = f[0] + s[1] + s[3] + s[5] + s[7] + s[9] + s[11] + s[13] + s[15] + s[17]
    inv_rho = 1.0 / rho
    ux = (d[1] + d[7] + d[9] + d[11] + d[13]) * inv_rho
    uy = (d[3] + d[7] - d[9] + d[15] + d[17]) * inv_rho
    uz = (d[5] + d[11] - d[13] + d[15] - d[17]) * inv_rho
    third = rho * (1.0 / 3.0)
    sxx = pxx - third - rho * ux * ux
    syy = pyy - third - rho * uy * uy
    szz = pzz - third - rho * uz * uz
    sxy = pxy - rho * ux * uy
    sxz = pxz - rho * ux * uz
    syz = pyz - rho * uy * uz
    contracted = sxx * sxx + syy * syy + szz * szz + 2.0 * (sxy * sxy + sxz * sxz + syz * syz)
    rate = 1.5 / 0.8 * inv_rho * jnp.sqrt(2.0 * contracted)
    scaled = 20.0 * rate
    viscosity = 0.01 + 0.09 * lax.rsqrt(jnp.sqrt(1.0 + scaled * scaled))
    omega = 1.0 / (3.0 * viscosity + 0.5)
    speed = 1.0 - 1.5 * (ux * ux + uy * uy + uz * uz)
    vel = (ux, uy, uz)
    out = [None] * Q
    out[0] = f[0] - (f[0] - WTS[0] * rho * speed) * omega
    for q in range(1, Q, 2):
        proj = None
        for comp, step in zip(vel, (CX[q], CY[q], CZ[q])):
            if step:
                term = comp if step > 0 else -comp
                proj = term if proj is None else proj + term
        scale = WTS[q] * rho
        even = scale * (speed + 4.5 * proj * proj)
        odd = scale * (3.0 * proj)
        out[q] = f[q] - (f[q] - (even + odd)) * omega
        out[q + 1] = f[q + 1] - (f[q + 1] - (even - odd)) * omega
    return out


def first_kernel(place_y_ref, pdf_ref, grains_ref, moves_ref, col_ref, near_ref, far_ref):
    lane = iota((ROWS, LANE), 1)
    col = collide([pdf_ref[q] for q in range(Q)])
    for q in range(Q):
        col_ref[q] = col[q]
    rims = []
    for chosen, edge in ((YUP, LANE - Z), (YDN, 0)):
        rim = jnp.zeros((ROWS, LANE), F32)
        for k, q in enumerate(chosen):
            moved = pltpu.roll(z_shift(col[q], CZ[q], lane), (k * Z - edge) % LANE, 1)
            rim = jnp.where(lane // Z == k, moved, rim)
        rims.append(rim)
    left = place_y_ref[0] % 2 == 0
    near_ref[0:ROWS, :] = jnp.where(left, rims[0], rims[1])
    far_ref[0:ROWS, :] = jnp.where(left, rims[1], rims[0])
    moves = moves_ref[...]
    count = moves.shape[1]
    matches = (iota((16, count), 0) == moves).astype(F32)
    earlier = (iota((count, count), 0) < iota((count, count), 1)).astype(F32).astype(BF16)
    before = dot_nn(matches.astype(BF16), earlier)
    rank = jnp.sum(matches * before, axis=0, keepdims=True).astype(I32)
    region = jnp.where(moves > 4, moves - 1, moves)
    target = jnp.where(moves == 4, -1, region * 8 + rank)
    placing = (iota((LANE, count), 0) == target).astype(F32).astype(BF16)
    own = grains_ref[:, 0, :]
    high, middle, low = split3(own)
    packed = dot_nt(high, placing) + dot_nt(middle, placing) + dot_nt(low, placing)
    for ref in (near_ref, far_ref):
        ref[ROWS : ROWS + GV, :] = packed
        ref[ROWS + GV :, :] = jnp.zeros((6, LANE), F32)


def y_shifted(q, plane, ylo, yhi, lane):
    plane = z_shift(plane, CZ[q], lane)
    if CY[q] == 1:
        k = YUP.index(q)
        return jnp.where(lane < Z, pltpu.roll(ylo, (LANE - k * Z) % LANE, 1), pltpu.roll(plane, Z, 1))
    if CY[q] == -1:
        k = YDN.index(q)
        return jnp.where(
            lane >= LANE - Z,
            pltpu.roll(yhi, (LANE - Z - k * Z) % LANE, 1),
            pltpu.roll(plane, LANE - Z, 1),
        )
    return plane


def from_pairs(place_y_ref, near_ref, far_ref, start, size):
    left = place_y_ref[0] % 2 == 0
    low = slice(start, start + size)
    high = slice(48 + start, 48 + start + size)
    far = far_ref[low, :]
    ylo = jnp.where(left, far, near_ref[low, :])
    yhi = jnp.where(left, near_ref[high, :], far)
    return ylo, yhi


def second_kernel(place_y_ref, col_ref, mine_ref, near_ref, far_ref, up_ref, dn_ref):
    lane = iota((8, LANE), 1)
    for ref, chosen, part, row in ((up_ref, XUP, 8, 7), (dn_ref, XDN, 0, 0)):
        ref[0:8, :] = jnp.zeros((8, LANE), F32)
        ylo, yhi = from_pairs(place_y_ref, near_ref, far_ref, part, 8)
        for k, q in enumerate(chosen):
            shifted = y_shifted(q, col_ref[q, part : part + 8, :], ylo, yhi, lane)
            ref[k : k + 1, :] = shifted[row : row + 1, :]
    grain_lane = iota((32, LANE), 1) // 8
    ylo, yhi = from_pairs(place_y_ref, near_ref, far_ref, ROWS, 32)
    joined = jnp.where(
        one_of(grain_lane, (2, 4, 7)), ylo, jnp.where(one_of(grain_lane, (0, 3, 5)), yhi, mine_ref[ROWS:, :])
    )
    up_ref[8:, :] = joined
    dn_ref[8:, :] = joined


def link_maps(place_x_ref, place_y_ref, link_ref, kept_parts, stay_parts, arrived_ref, spread_ref, term_ref, pick_ref):
    toward = []
    for bx in range(2):
        cell = link_ref[0, bx : bx + 1, :]
        direction = link_ref[1, bx : bx + 1, :]
        slot = link_ref[2, bx : bx + 1, :]
        links = cell.shape[1]
        side = iota((1, links), 1) // 256

        def component(table):
            plus = one_of(direction, [q for q in range(Q) if table[q] == 1])
            minus = one_of(direction, [q for q in range(Q) if table[q] == -1])
            return jnp.where(plus, 1.0, jnp.where(minus, -1.0, 0.0))

        steps = [component(table) for table in (CX, CY, CZ)]
        corner = (
            (place_x_ref[0] * 2 + bx) * E + cell // (E * Z),
            (place_y_ref[0] * 2 + side) * E + cell // Z % E,
            cell % Z,
        )
        row = cell // (E * Z)
        terms = [c.astype(F32) + 0.5 * step for c, step in zip(corner, steps)] + steps
        terms += [jnp.where(direction <= 6, W6_AXIS, W6_DIAG), row.astype(F32)]
        for k, term in enumerate(terms):
            term_ref[bx, k : k + 1, :] = term
        kept = (iota((256, links), 0) == slot).astype(F32).astype(BF16)
        arrived = (iota((LANE, links), 0) + 256 == slot).astype(F32).astype(BF16)
        arrived_ref[bx] = arrived
        picked = dot_nn(kept_parts, kept) + dot_nn(stay_parts, arrived)
        pick_ref[bx] = picked[0:16] + picked[16:32] + picked[32:48]
        spread = (iota((LANE, links), 0) == side * 64 + cell % 64).astype(F32).astype(BF16)
        spread_ref[bx] = spread
        left = jnp.where(iota((8, links), 0) == row, direction.astype(F32), 0.0).astype(BF16)
        toward.append(dot_nt(left, spread))
    return jnp.concatenate(toward, axis=0)


def block_order(scratch_ref, plane):
    low_half = iota((8, LANE), 1) < 64
    scratch_ref[...] = plane
    even = scratch_ref[pl.ds(0, 8, stride=2), :]
    odd = scratch_ref[pl.ds(1, 8, stride=2), :]
    first = jnp.where(low_half, even, pltpu.roll(odd, 64, 1))
    second = jnp.where(low_half, pltpu.roll(even, 64, 1), odd)
    return first, second


def prepare_kernel(
    place_x_ref, place_y_ref, link_ref, col_ref, near_ref, far_ref, mine_ref, grains_ref, moves_ref, after_ref,
    plane_ref, value_ref, toward_ref, pick_ref, own_ref, arrived_ref, spread_ref, term_ref, scratch_ref,
):
    del after_ref
    lane = iota((ROWS, LANE), 1)
    kept = jnp.where(moves_ref[...] == 4, grains_ref[:, 0, :], 0.0)
    own_ref[...] = kept
    stay = jnp.where(one_of(iota((16, LANE), 1) // 8, (3, 4)), mine_ref[8:24, :], 0.0)
    kept_parts = jnp.concatenate(split3(kept[0:16]), axis=0)
    stay_parts = jnp.concatenate(split3(stay), axis=0)
    toward = link_maps(
        place_x_ref, place_y_ref, link_ref, kept_parts, stay_parts, arrived_ref, spread_ref, term_ref, pick_ref
    )
    for half, part in enumerate(block_order(scratch_ref.at[0], toward)):
        toward_ref[half] = part.astype(I32)
    ylo, yhi = from_pairs(place_y_ref, near_ref, far_ref, 0, ROWS)
    for q in range(Q):
        plane = y_shifted(q, col_ref[q], ylo, yhi, lane)
        if CX[q]:
            plane = pltpu.roll(plane, CX[q] % ROWS, 0)
        for ref, given in ((plane_ref, plane), (value_ref, col_ref[OPP[q]])):
            for half, part in enumerate(block_order(scratch_ref.at[q % 4 + (4 if ref is value_ref else 0)], given)):
                ref[q, half] = part


def table_kernel(mine_ref, xlo_ref, xhi_ref, own_ref, table_ref):
    grain_lane = iota((32, LANE), 1) // 8
    arrived = jnp.where(
        one_of(grain_lane, (5, 6, 7)),
        xlo_ref[8:, :],
        jnp.where(one_of(grain_lane, (0, 1, 2)), xhi_ref[8:, :], mine_ref[8:, :]),
    )
    table_ref[:, 0, 0:256] = own_ref[...]
    table_ref[:, 0, 256:320] = arrived[0:GV, 0:64]


def finish_kernel(
    owner_ref, plane_ref, value_ref, toward_ref, xlo_ref, xhi_ref, pick_ref,
    arrived_ref, spread_ref, term_ref, send_ref, scratch_ref,
):
    send_ref[...] = jnp.zeros(send_ref.shape, F32)
    grain_lane = iota((16, LANE), 1) // 8
    moved = jnp.where(
        one_of(grain_lane, (5, 6, 7)),
        xlo_ref[8:24, :],
        jnp.where(one_of(grain_lane, (0, 1, 2)), xhi_ref[8:24, :], 0.0),
    )
    moved_parts = jnp.concatenate(split3(moved), axis=0)
    corrections = []
    for bx in range(2):
        picked = dot_nn(moved_parts, arrived_ref[bx])
        g = pick_ref[bx] + (picked[0:16] + picked[16:32] + picked[32:48])
        mid_x, mid_y, mid_z, step_x, step_y, step_z, scale, at = (term_ref[bx, k : k + 1, :] for k in range(8))
        rel_x = mid_x - g[0:1]
        rel_y = mid_y - g[1:2]
        rel_z = mid_z - g[2:3]
        wall_x = g[3:4] + g[7:8] * rel_z - g[8:9] * rel_y
        wall_y = g[4:5] + g[8:9] * rel_x - g[6:7] * rel_z
        wall_z = g[5:6] + g[6:7] * rel_y - g[7:8] * rel_x
        correction = scale * (step_x * wall_x + step_y * wall_y + step_z * wall_z)
        here = iota((8, correction.shape[1]), 0) == at.astype(I32)
        left = jnp.concatenate(
            [jnp.where(here, part.astype(F32), 0.0) for part in split3(correction)], axis=0
        ).astype(BF16)
        dense = dot_nt(left, spread_ref[bx])
        corrections.append(dense[0:8] + dense[8:16] + dense[16:24])
    correction = jnp.concatenate(corrections, axis=0)
    correction = block_order(scratch_ref, correction)
    base = [owner_ref[n // 2, n % 2] * Q for n in range(4)]
    low_half = iota((8, LANE), 1) < 64
    row = iota((8, LANE), 0)
    first_row = jnp.logical_and(row == 0, low_half)
    last_row = jnp.logical_and(row == 7, jnp.logical_not(low_half))
    turned_low = pltpu.roll(xlo_ref[0:8, :], 64, 1)
    turned_high = pltpu.roll(xhi_ref[0:8, :], 64, 1)
    for q in range(Q):
        for half in range(2):
            part = plane_ref[q, half]
            if CX[q] == 1:
                k = XUP.index(q)
                edge = turned_low[k : k + 1] if half else xlo_ref[k : k + 1, :]
                part = jnp.where(first_row, edge, part)
            elif CX[q] == -1:
                k = XDN.index(q)
                edge = xhi_ref[k : k + 1, :] if half else turned_high[k : k + 1]
                part = jnp.where(last_row, edge, part)
            if q:
                part = jnp.where(toward_ref[half] == OPP[q], value_ref[q, half] - correction[half], part)
            send_ref[base[half] + q] = part[0:4]
            send_ref[base[2 + half] + q] = part[4:8]


VMEM = pl.BlockSpec(memory_space=pltpu.VMEM)
SMEM = pl.BlockSpec(memory_space=pltpu.SMEM)


def ring(axis, step):
    count = lax.axis_size(axis)
    return [(i, (i + step) % count) for i in range(count)]


def near(*arrays):
    return tuple(pltpu.with_memory_space_constraint(a, pltpu.VMEM) for a in arrays)


def chip(*dims, dtype=F32):
    return pltpu.VMEM(dims, dtype)


def body(pdf, grains, grain_moves, owner_map, link_lists):
    group = lax.axis_size("gx")
    place_x = lax.axis_index("gx").astype(I32).reshape(1)
    place_y = lax.axis_index("gy").astype(I32).reshape(1)
    links = link_lists.shape[2]
    col, near_msg, far_msg = pl.pallas_call(
        first_kernel,
        out_shape=(chip(Q, ROWS, LANE), chip(48, LANE), chip(48, LANE)),
        in_specs=[SMEM] + [VMEM] * 3,
        out_specs=(VMEM,) * 3,
        name="collide_pack",
    )(place_y, pdf, grains, grain_moves)
    columns = lax.axis_size("gy")
    far_pair = lax.ppermute(far_msg, "gy", [(i, (i + 2 * (i % 2) - 1) % columns) for i in range(columns)])
    near_pair = lax.all_gather(
        near_msg, "gy", axis=0, tiled=True, axis_index_groups=[[i, i + 1] for i in range(0, columns, 2)]
    )
    x_up, x_dn = pl.pallas_call(
        second_kernel,
        out_shape=(chip(40, LANE), chip(40, LANE)),
        in_specs=[SMEM] + [VMEM] * 4,
        out_specs=(VMEM,) * 2,
        name="x_messages",
    )(place_y, *near(col, near_msg, near_pair, far_pair))
    xlo = lax.ppermute(x_up, "gx", ring("gx", 1))
    xhi = lax.ppermute(x_dn, "gx", ring("gx", -1))
    plane, value, toward, pick, own, arrived, spread, terms = pl.pallas_call(
        prepare_kernel,
        out_shape=(
            chip(Q, 2, 8, LANE),
            chip(Q, 2, 8, LANE),
            chip(2, 8, LANE, dtype=I32),
            chip(2, 16, links),
            chip(GV, 256),
            chip(2, LANE, links, dtype=BF16),
            chip(2, LANE, links, dtype=BF16),
            chip(2, 8, links),
        ),
        in_specs=[SMEM, SMEM] + [VMEM] * 8,
        out_specs=(VMEM,) * 8,
        scratch_shapes=[pltpu.VMEM((8, ROWS, LANE), F32)],
        cost_estimate=pl.CostEstimate(flops=4_000_000, bytes_accessed=1_000_000, transcendentals=0),
        name="prepare",
    )(place_x, place_y, link_lists, *near(col, near_pair, far_pair, x_up), grains, grain_moves, *near(x_dn))
    send = pl.pallas_call(
        finish_kernel,
        out_shape=jax.ShapeDtypeStruct((group * Q, 4, LANE), F32),
        in_specs=[SMEM] + [VMEM] * 9,
        out_specs=VMEM,
        scratch_shapes=[pltpu.VMEM((ROWS, LANE), F32)],
        name="finish_blocks",
    )(owner_map, *near(plane, value, toward, xlo, xhi, pick, arrived, spread, terms))
    table = pl.pallas_call(
        table_kernel,
        out_shape=jax.ShapeDtypeStruct((GV, 1, 320), F32),
        in_specs=[VMEM] * 4,
        out_specs=VMEM,
        name="grain_table",
    )(*near(x_up, xlo, xhi, own))
    out = lax.all_to_all(send.reshape(group, 1, Q, 512), "gx", split_axis=0, concat_axis=0, tiled=True)
    return (out, table)


def solution(mesh):
    in_specs = (
        P(None, "gx", "gy"),
        P(None, "gx", "gy"),
        P("gx", "gy"),
        P("gx", "gy"),
        P(None, "gx", "gy"),
    )
    out_specs = (P("gx", "gy", None, None), P(None, "gx", "gy"))
    return jax.shard_map(body, mesh=mesh, in_specs=in_specs, out_specs=out_specs, check_vma=False)
```
